32 devices in a mesh: dp: 8 (over z, x), seq: 4 (over y, core).
Axes of the slice: x: 2, y: 2, z: 4, core: 2. Of those that a mesh axis runs over, the one named last changes fastest.
Arguments:
- residual: bfloat16 [8, 1024, 2048], P('dp', 'seq'), may hold values from -64 to 64
- cotangent: bfloat16 [8, 1024, 2048], P('dp', 'seq'), may hold values from -6 to 6
- attn_gain: bfloat16 [2048], P(('dp', 'seq')), may hold values from 0.099609375 to 1.8984375
- query_weight: bfloat16 [2048, 2048], P(('dp', 'seq')), may hold values from -0.1875 to 0.1875
- key_weight: bfloat16 [2048, 256], P(('dp', 'seq')), may hold values from -0.125 to 0.125
- value_weight: bfloat16 [2048, 256], P(('dp', 'seq')), may hold values from -0.125 to 0.125
- out_weight: bfloat16 [2048, 2048], P(('dp', 'seq')), may hold values from -1 to 1
- ffn_gain: bfloat16 [2048], P(('dp', 'seq')), may hold values from 0.099609375 to 1.8984375
- gate_weight: bfloat16 [2048, 5632], P('dp', 'seq'), may hold values from -0.125 to 0.125
- up_weight: bfloat16 [2048, 5632], P('dp', 'seq'), may hold values from -0.125 to 0.125
- down_weight: bfloat16 [2048, 5632], P('dp', 'seq'), may hold values from -0.078125 to 0.078125
Outputs:
- output: bfloat16 [8, 1024, 2048], P('dp', 'seq')
- grad_input: float32 [8, 1024, 2048], P('dp', 'seq')
- grad_attn_gain: float32 [2048], P(('dp', 'seq'))
- grad_query_weight: float32 [2048, 2048], P(('dp', 'seq'))
- grad_key_weight: float32 [2048, 256], P(('dp', 'seq'))
- grad_value_weight: float32 [2048, 256], P(('dp', 'seq'))
- grad_out_weight: float32 [2048, 2048], P(('dp', 'seq'))
- grad_ffn_gain: float32 [2048], P(('dp', 'seq'))
- grad_gate_weight: float32 [2048, 5632], P('dp', 'seq')
- grad_up_weight: float32 [2048, 5632], P('dp', 'seq')
- grad_down_weight: float32 [2048, 5632], P('dp', 'seq')
- rms_stats: float32 [4], replicated
The draws below stay inside these ranges and needn't reach their ends.
All inputs are finite; a program needn't handle non-finite values.
Results may differ from the reference program's by a relative error of at most 0.023.
Values may be sent and summed in bfloat16 or wider, within the bound.
No kernel may reach another device: no remote copies, remote signals or barrier semaphores. Data moves between devices by JAX's collectives and lax.ppermute only.
A program may use at most 384 MiB of HBM per device.

```python
import math
import jax
import jax.numpy as jnp
from jax import lax

D = 2048
H = 32
KV = 4
HD = 64
FF = 5632
LEN = 1024
SEQS = 8


def draw_residual(key, part):
    keys_list = jax.random.split(jax.random.fold_in(key, 11), 7)
    row_total = SEQS * LEN
    fraction = jnp.arange(row_total, dtype=jnp.float32) / max(row_total - 1, 1)
    spread = jax.random.uniform(keys_list[0], (row_total,), jnp.float32)
    row_scale = 0.15 * jnp.exp(math.log(3.0) * fraction + math.log(3.3) * spread)
    col_scale = jnp.exp(math.log(0.4) + math.log(10.0) * jax.random.uniform(keys_list[1], (D,), jnp.float32))
    values = jnp.clip(jax.random.normal(keys_list[2], (row_total, D), jnp.float32), -4.5, 4.5)
    values = values * (1.0 / math.sqrt(2.0)) * row_scale[:, None] * col_scale[None, :]
    chosen = jax.random.permutation(keys_list[4], D)[:2]
    signs = (2 * jax.random.randint(keys_list[5], (2,), 0, 2) - 1).astype(jnp.float32)
    jitter = jax.random.uniform(keys_list[6], (row_total, 2), jnp.float32, 0.8, 1.2)
    columns = jnp.arange(D)
    first_col = (columns == chosen[0]).astype(jnp.float32) * signs[0]
    second_col = (columns == chosen[1]).astype(jnp.float32) * signs[1]
    special = jitter[:, 0:1] * first_col[None, :] + jitter[:, 1:2] * second_col[None, :]
    magnitude = math.sqrt(0.86 * D)
    values = values + magnitude * row_scale[:, None] * special
    values = jnp.clip(values, -64.0, 64.0)
    return values.reshape(SEQS, LEN, D).astype(jnp.bfloat16)


def spiked(result, own_key, source, target, shards_of, factor):
    owner, partner = [(jnp.arange(result.shape[axis_at]) // (result.shape[axis_at] // shards_of)).reshape([-1 if axis == axis_at else 1 for axis in range(result.ndim)]) for axis_at in (source, target)]
    chosen = jax.random.permutation(own_key, shards_of)[partner]
    strong = (owner == chosen) | (owner == (partner + shards_of // 2) % shards_of)
    return jnp.where(strong, factor * result, result)


def block_levels(rng, shape, cuts, least, largest):
    def one(axis_at, shards_of):
        draws = jax.random.uniform(jax.random.fold_in(jax.random.fold_in(rng, 6), axis_at), (shards_of,), jnp.float32, least / len(cuts), largest / len(cuts))
        return jnp.repeat(jnp.exp(draws), shape[axis_at] // shards_of).reshape((-1,) + (1,) * (len(shape) - axis_at - 1))

    level = one(*cuts[0])
    for cut in cuts[1:]:
        level = level * one(*cut)
    return level


def scatter_about(key, shape, scale, limit, cuts=(), held_as=jnp.bfloat16):
    entries = jax.random.normal(key, shape, jnp.float32) * scale
    if len(cuts) > 0:
        entries = block_levels(key, shape, cuts, -0.22, 0.18) * entries
    return jnp.clip(entries, min=-limit, max=limit).astype(held_as)


def noise_with(own_key, dims, scale, limit, shards, heavy, kind=jnp.bfloat16):
    values = scale * jax.random.normal(own_key, dims, jnp.float32)
    if shards:
        values = values * block_levels(own_key, dims, shards, -0.22, 0.18)
    return jnp.clip(spiked(values, jax.random.fold_in(own_key, 3), *heavy), -limit, limit).astype(kind)


def setup_inputs(seed: int = 0) -> dict:
    seeds = jax.random.split(jax.random.key(seed), 12)
    return {
        "residual": draw_residual(jax.random.fold_in(seeds[11], 71), 0),
        "cotangent": noise_with(seeds[1], (SEQS, LEN, D), 1.0, 6.0, ((0, 8), (1, 4)), (0, 2, 8, 2.0)),
        "attn_gain": jnp.clip(1.0 + 0.18 * jax.random.normal(seeds[2], (D,), jnp.float32), 0.099609375, 1.8984375).astype(jnp.bfloat16),
        "query_weight": scatter_about(seeds[3], (D, H * HD), (D // 2) ** -0.5, 0.1875, ((0, 32),)),
        "key_weight": scatter_about(seeds[4], (D, KV * HD), D ** -0.5, 0.125, ((0, 32),)),
        "value_weight": scatter_about(seeds[5], (D, KV * HD), D ** -0.5, 0.125, ((0, 32),)),
        "out_weight": scatter_about(seeds[6], (H * HD, D), (max(1, H * HD * 16 // LEN)) ** -0.5, 1.0, ((0, 32),)),
        "ffn_gain": jnp.clip(1.0 + 0.18 * jax.random.normal(seeds[7], (D,), jnp.float32), 0.099609375, 1.8984375).astype(jnp.bfloat16),
        "gate_weight": scatter_about(seeds[8], (D, FF), D ** -0.5, 0.125, ((0, 8), (1, 4))),
        "up_weight": scatter_about(seeds[9], (D, FF), D ** -0.5, 0.125, ((0, 8), (1, 4))),
        "down_weight": scatter_about(seeds[10], (D, FF), FF ** -0.5, 0.078125, ((0, 8), (1, 4))),
    }


EPS = 1e-05
HIGH = lax.Precision.HIGHEST

@jax.custom_vjp
def low(v):
    return lax.optimization_barrier(v.astype(jnp.bfloat16)).astype(jnp.float32)

@jax.custom_vjp
def low_back(v):
    return v

def low_keep(v):
    return (low(v), None)

def low_pass(kept, grad):
    return (grad,)

def back_keep(v):
    return (v, None)

def back_low(kept, grad):
    return (low(grad),)
low.defvjp(low_keep, low_pass)
low_back.defvjp(back_keep, back_low)

def matmul(left, right):
    return jnp.dot(left, right, precision=HIGH, preferred_element_type=jnp.float32)

def rotary(values, positions):
    half_width = values.shape[-1] // 2
    freq_table = jnp.exp(-math.log(10000.0) * 2.0 * jnp.arange(half_width, dtype=jnp.float32) / values.shape[-1])
    angles = positions[:, None] * freq_table[None, :]
    cosine = jnp.cos(angles)[:, None, :]
    sine = jnp.sin(angles)[:, None, :]
    first = values[..., :half_width]
    second = values[..., half_width:]
    return jnp.concatenate([first * cosine - second * sine, second * cosine + first * sine], axis=-1)

def group_attention(inputs):
    queries, keys_all, values_all = inputs
    length = queries.shape[0]
    scores = jnp.einsum('qgd,td->gqt', queries, keys_all, precision=HIGH) * (1.0 / math.sqrt(HD))
    scores = low_back(scores)
    allowed = jnp.arange(length)[None, :] <= jnp.arange(length)[:, None]
    scores = jnp.where(allowed[None], scores, -1e+30)
    weights = jax.nn.softmax(scores, axis=-1)
    return jnp.einsum('gqt,td->qgd', low(weights), values_all, precision=HIGH)

def block_forward(stream, params):
    gain_one, w_query, w_key, w_value, w_out, gain_two, w_gate, w_up, w_down = params
    length = stream.shape[0]
    positions = jnp.arange(length).astype(jnp.float32)
    inverse_one = lax.rsqrt(lax.optimization_barrier(jnp.mean(stream * stream, axis=-1, keepdims=True)) + EPS)
    normed_one = low(stream * inverse_one * gain_one)
    queries = low_back(matmul(normed_one, w_query)).reshape(length, H, HD)
    keys_all = low_back(matmul(normed_one, w_key)).reshape(length, KV, HD)
    values_all = low_back(matmul(normed_one, w_value)).reshape(length, KV, HD)
    queries = low(rotary(queries, positions))
    keys_all = low(rotary(keys_all, positions))
    values_all = low(values_all)
    grouped = jnp.transpose(queries.reshape(length, KV, H // KV, HD), (1, 0, 2, 3))
    heads_out = lax.map(jax.checkpoint(group_attention), (grouped, jnp.transpose(keys_all, (1, 0, 2)), jnp.transpose(values_all, (1, 0, 2))))
    attended = jnp.transpose(heads_out, (1, 0, 2, 3)).reshape(length, H * HD)
    attended = low_back(low(attended))
    branch = low_back(matmul(attended, w_out))
    middle = stream + branch
    inverse_two = lax.rsqrt(lax.optimization_barrier(jnp.mean(middle * middle, axis=-1, keepdims=True)) + EPS)
    normed_two = low(middle * inverse_two * gain_two)
    gate_pre = low_back(matmul(normed_two, w_gate))
    up_pre = low_back(matmul(normed_two, w_up))
    hidden = low(jax.nn.silu(gate_pre) * up_pre)
    feed_out = low_back(matmul(hidden, w_down.T))
    return (middle + feed_out, (branch, feed_out))

def reference(residual, cotangent, attn_gain, query_weight, key_weight, value_weight, out_weight, ffn_gain, gate_weight, up_weight, down_weight):
    params = tuple((weight_arg.astype(jnp.float32) for weight_arg in (attn_gain, query_weight, key_weight, value_weight, out_weight, ffn_gain, gate_weight, up_weight, down_weight)))
    zeros_all = tuple((jnp.zeros_like(weight_arg) for weight_arg in params))

    def step(carry, item):
        grad_totals, square_sums = carry
        seq_rows, seq_cot = item
        stream = seq_rows.astype(jnp.float32)
        total_out, pullback, extras = jax.vjp(block_forward, stream, params, has_aux=True)
        branch, feed_out = extras
        grad_rows, grad_params = pullback(seq_cot.astype(jnp.float32))
        grad_totals = tuple((old_grad + new_grad for old_grad, new_grad in zip(grad_totals, grad_params)))
        squares = jnp.stack([jnp.sum(stream * stream), jnp.sum(branch * branch), jnp.sum(feed_out * feed_out), jnp.sum(total_out * total_out)])
        return ((grad_totals, square_sums + squares), (total_out.astype(jnp.bfloat16), grad_rows))
    (grad_totals, square_sums), (outputs, grad_rows) = lax.scan(step, (zeros_all, jnp.zeros((4,), jnp.float32)), (residual, cotangent))
    rms_stats = jnp.sqrt(square_sums / (SEQS * LEN * D))
    return (outputs, grad_rows, grad_totals[0], grad_totals[1], grad_totals[2], grad_totals[3], grad_totals[4], grad_totals[5], grad_totals[6], grad_totals[7], grad_totals[8], rms_stats)
```

```python
import math

import jax
import jax.numpy as jnp
from jax import lax
from jax.sharding import PartitionSpec as P

HD = 64
EPS = 1e-05
AXES = ("dp", "seq")
BF = jnp.bfloat16
F32 = jnp.float32


def contract(left, right, left_dim, right_dim):
    return lax.dot_general(
        left, right, (((left_dim,), (right_dim,)), ((), ())), preferred_element_type=F32
    )


def flip(value, mask):
    count = lax.axis_size("dp") * lax.axis_size("seq")
    return lax.ppermute(value, AXES, [(k, k ^ mask) for k in range(count)])


def column_groups():
    size = lax.axis_size("dp")
    return [list(range(start, size, 2)) for start in range(2)]


def gather_z(value):
    return lax.all_gather(value, "dp", axis=0, tiled=True, axis_index_groups=column_groups())


def scatter_z(value):
    return lax.psum_scatter(
        value, "dp", scatter_dimension=0, tiled=True, axis_index_groups=column_groups()
    )


def pick(is_first, own, other):
    return (jnp.where(is_first, own, other), jnp.where(is_first, other, own))


def gather_eight(block):
    half = block.shape[0] // 2
    top, low = block[:half], block[half:]
    top_x = flip(top, 4)
    low_y = flip(low, 2)
    tops_y = flip(jnp.concatenate([top, top_x], axis=0), 2)
    lows_x = flip(jnp.concatenate([low, low_y], axis=0), 4)
    chip = jnp.concatenate(
        [
            block,
            tops_y[:half],
            low_y,
            top_x,
            lows_x[:half],
            tops_y[half:],
            lows_x[half:],
        ],
        axis=0,
    )
    other = flip(chip, 1)
    return jnp.concatenate([chip, other], axis=0)


def scatter_eight(partial):
    rows = partial.shape[0] // 8
    half = rows // 2
    mine, theirs = partial[: 4 * rows], partial[4 * rows :]
    chip = (mine + flip(theirs.astype(BF), 1).astype(F32)).reshape(4, 2, half, -1)
    tops, lows = chip[:, 0], chip[:, 1]
    got_x = flip(tops[2:].astype(BF), 4).astype(F32)
    got_y = flip(lows[1::2].astype(BF), 2).astype(F32)
    tops = tops[:2] + got_x
    lows = lows[0::2] + got_y
    got_y = flip(tops[1].astype(BF), 2).astype(F32)
    got_x = flip(lows[1].astype(BF), 4).astype(F32)
    return jnp.concatenate([tops[0] + got_y, lows[0] + got_x], axis=0)


def gather_seq(block):
    rank = lax.axis_index("seq")
    across = flip(block, 2)
    core = flip(block, 1)
    core_across = flip(across, 1)
    result = jnp.zeros((4,) + block.shape, block.dtype)
    for mask, part in enumerate((block, core, across, core_across)):
        result = lax.dynamic_update_index_in_dim(result, part, rank ^ mask, 0)
    return result.reshape((4 * block.shape[0],) + block.shape[1:])


def scatter_seq(partial):
    rank = lax.axis_index("seq")
    rows = partial.shape[0] // 4
    parts = partial.reshape((4, rows) + partial.shape[1:])
    take = lambda mask: lax.dynamic_index_in_dim(parts, rank ^ mask, 0, keepdims=False)
    got = flip(jnp.stack([take(1), take(3)]).astype(BF), 1).astype(F32)
    across = flip((take(2) + got[1]).astype(BF), 2).astype(F32)
    return take(0) + got[0] + across


def rotary(values, positions, direction):
    half_width = values.shape[-1] // 2
    freq_table = jnp.exp(
        -math.log(10000.0) * 2.0 * jnp.arange(half_width, dtype=F32) / values.shape[-1]
    )
    angles = positions[:, None] * freq_table[None, :]
    cosine = jnp.cos(angles)[:, None, :]
    sine = direction * jnp.sin(angles)[:, None, :]
    first = values[..., :half_width]
    second = values[..., half_width:]
    return jnp.concatenate(
        [first * cosine - second * sine, second * cosine + first * sine], axis=-1
    )


def block_scores(queries, keys_all, row_start, row_count):
    scores = jnp.einsum("qgd,td->gqt", queries, keys_all, preferred_element_type=F32) * (
        1.0 / math.sqrt(HD)
    )
    allowed = jnp.arange(keys_all.shape[0])[None, :] <= (row_start + jnp.arange(row_count))[:, None]
    return (jnp.where(allowed, scores, -1e30), allowed)


def attend(queries, keys_all, values_all):
    length = queries.shape[0]
    blocks = max(1, length // 512)
    block_rows = length // blocks
    outputs = []
    totals = []
    for block_index in range(blocks):
        row_start = block_index * block_rows
        row_end = row_start + block_rows
        scores, allowed = block_scores(
            queries[row_start:row_end], keys_all[:row_end], row_start, block_rows
        )
        highest = jnp.max(scores, axis=-1, keepdims=True)
        weights = jnp.exp(scores - highest)
        weight_sum = jnp.sum(weights, axis=-1, keepdims=True)
        prob_low = (weights / weight_sum).astype(BF)
        mixed = jnp.einsum("gqt,td->qgd", prob_low, values_all[:row_end], preferred_element_type=F32)
        outputs.append(mixed.reshape(block_rows, -1).astype(BF))
        totals.append(highest + jnp.log(weight_sum))
    return (jnp.concatenate(outputs, axis=0), totals)


def attend_back(queries, keys_all, values_all, grad_outs, totals):
    length = queries.shape[0]
    blocks = max(1, length // 512)
    block_rows = length // blocks
    scale_value = 1.0 / math.sqrt(HD)
    grad_keys = jnp.zeros(keys_all.shape, F32)
    grad_values = jnp.zeros(values_all.shape, F32)
    query_parts = []
    for block_index in range(blocks):
        row_start = block_index * block_rows
        row_end = row_start + block_rows
        query_block = queries[row_start:row_end]
        grad_block = grad_outs[row_start:row_end]
        scores, allowed = block_scores(query_block, keys_all[:row_end], row_start, block_rows)
        weights = jnp.where(allowed, jnp.exp(scores - totals[block_index]), 0.0)
        prob_low = weights.astype(BF)
        grad_probs = jnp.einsum(
            "qgd,td->gqt", grad_block, values_all[:row_end], preferred_element_type=F32
        )
        inner = jnp.sum(weights * grad_probs, axis=-1, keepdims=True)
        grad_scores = (weights * (grad_probs - inner)).astype(BF)
        query_parts.append(
            jnp.einsum("gqt,td->qgd", grad_scores, keys_all[:row_end], preferred_element_type=F32)
            * scale_value
        )
        padding = ((0, length - row_end), (0, 0))
        key_term = (
            jnp.einsum("gqt,qgd->td", grad_scores, query_block, preferred_element_type=F32)
            * scale_value
        )
        value_term = jnp.einsum("gqt,qgd->td", prob_low, grad_block, preferred_element_type=F32)
        grad_keys = grad_keys + jnp.pad(key_term, padding)
        grad_values = grad_values + jnp.pad(value_term, padding)
    return (jnp.concatenate(query_parts, axis=0), grad_keys, grad_values)


def per_device(
    residual,
    cotangent,
    attn_gain,
    query_weight,
    key_weight,
    value_weight,
    out_weight,
    ffn_gain,
    gate_weight,
    up_weight,
    down_weight,
):
    dp_size = lax.axis_size("dp")
    seq_size = lax.axis_size("seq")
    columns = dp_size // 2
    dp_rank = lax.axis_index("dp")
    rank = lax.axis_index("seq")
    is_first = dp_rank % 2 == 0
    tokens = residual.shape[1]
    width = residual.shape[2]
    rows_small = query_weight.shape[0]
    rows_ffn = gate_weight.shape[0]
    head_cols = query_weight.shape[1] // seq_size
    pair_cols = key_weight.shape[1] // seq_size
    length = tokens * seq_size

    own_rows = residual[0]
    stream = own_rows.astype(F32)
    inverse_one = lax.rsqrt(jnp.mean(stream * stream, axis=-1, keepdims=True) + EPS)
    cot_rows = cotangent[0]

    gain_one = attn_gain.astype(F32)[:, None]
    own_qkv = jnp.concatenate(
        [
            query_weight.reshape(rows_small, seq_size, head_cols),
            key_weight.reshape(rows_small, seq_size, pair_cols),
            value_weight.reshape(rows_small, seq_size, pair_cols),
        ],
        axis=2,
    ).astype(F32)
    send_qkv = (own_qkv * gain_one[:, :, None]).astype(BF)
    part_qkv = lax.all_to_all(send_qkv, "seq", split_axis=1, concat_axis=0, tiled=True)
    part_qkv = part_qkv.reshape(seq_size * rows_small, -1)
    count = dp_size * seq_size
    out_moves = [(k, (k % dp_size) * seq_size + k // dp_size) for k in range(count)]
    part_out = lax.ppermute(out_weight, AXES, out_moves)

    def over_x(part, rows):
        column = gather_z(part)
        first, second = pick(is_first, column, flip(column, 4))
        both = jnp.stack([first.reshape(columns, rows, -1), second.reshape(columns, rows, -1)], 1)
        return both.reshape(dp_size * rows, -1)

    w_qkv = over_x(part_qkv, seq_size * rows_small)
    w_out = over_x(part_out, rows_small)

    slots = jnp.zeros((seq_size, ffn_gain.shape[0]), F32)
    slots = lax.dynamic_update_index_in_dim(slots, ffn_gain.astype(F32), rank, 0)
    slots = slots + flip(slots, 1)
    slots = slots + flip(slots, 2)
    gain_two = slots.reshape(rows_ffn, 1)
    hidden_half = gate_weight.shape[1] // 2

    def halves(weight):
        left, right = weight[:, :hidden_half], weight[:, hidden_half:]
        mine = jnp.where(is_first, left, right)
        theirs = jnp.where(is_first, right, left)
        return jnp.concatenate(pick(is_first, mine, flip(theirs, 4)), axis=0)

    gate_scaled = (gate_weight.astype(F32) * gain_two).astype(BF)
    up_scaled = (up_weight.astype(F32) * gain_two).astype(BF)
    w_gate = gather_z(halves(gate_scaled))
    w_up = gather_z(halves(up_scaled))
    w_down = gather_z(halves(down_weight))

    stream_all = gather_seq(own_rows).astype(F32)
    inverse_all = lax.rsqrt(jnp.mean(stream_all * stream_all, axis=-1, keepdims=True) + EPS)
    unit_one = (stream_all * inverse_all).astype(BF)
    qkv = jnp.dot(unit_one, w_qkv, preferred_element_type=F32)
    positions = jnp.arange(length).astype(F32)
    queries = rotary(qkv[:, :head_cols].reshape(length, -1, HD), positions, 1.0).astype(BF)
    keys_all = rotary(qkv[:, head_cols : head_cols + HD].reshape(length, 1, HD), positions, 1.0)
    keys_all = keys_all[:, 0].astype(BF)
    values_all = qkv[:, head_cols + HD :].astype(BF)
    attended, totals = attend(queries, keys_all, values_all)
    branch = scatter_seq(jnp.dot(attended, w_out, preferred_element_type=F32))
    middle = stream + branch
    inverse_two = lax.rsqrt(jnp.mean(middle * middle, axis=-1, keepdims=True) + EPS)

    unit_two = gather_eight((middle * inverse_two).astype(BF))
    cot_all = gather_eight(cot_rows)
    gate_pre = jnp.dot(unit_two, w_gate, preferred_element_type=F32)
    up_pre = jnp.dot(unit_two, w_up, preferred_element_type=F32)
    gate_sigmoid = jax.nn.sigmoid(gate_pre)
    silu_gate = gate_pre * gate_sigmoid
    hidden = (silu_gate * up_pre).astype(BF)
    feed = scatter_eight(contract(hidden, w_down, 1, 1))
    total_out = middle + feed
    grad_hidden = jnp.dot(cot_all, w_down, preferred_element_type=F32)
    grad_silu = gate_sigmoid * (1.0 + gate_pre * (1.0 - gate_sigmoid))
    grad_gate = (grad_hidden * up_pre * grad_silu).astype(BF)
    grad_up = (grad_hidden * silu_gate).astype(BF)
    grad_unit_two = scatter_eight(contract(grad_gate, w_gate, 1, 1) + contract(grad_up, w_up, 1, 1))

    def scatter_ffn(left, right):
        term = scatter_z(contract(left, right, 0, 0).astype(BF))
        first, second = term[:rows_ffn], term[rows_ffn:]
        mine = jnp.where(is_first, first, second)
        theirs = jnp.where(is_first, second, first)
        return jnp.concatenate(pick(is_first, mine, flip(theirs, 4)), axis=1).astype(F32)

    grad_down_w = scatter_ffn(cot_all, hidden)
    grad_gate_w = scatter_ffn(unit_two, grad_gate)
    grad_up_w = scatter_ffn(unit_two, grad_up)
    gain_rows = jnp.sum(
        grad_gate_w * gate_weight.astype(F32) + grad_up_w * up_weight.astype(F32), axis=1
    )
    gain_rows = gain_rows + flip(gain_rows, 1)
    gain_rows = gain_rows + flip(gain_rows, 2)
    grad_ffn_gain = lax.dynamic_slice_in_dim(gain_rows, rank * rows_small, rows_small)
    grad_gate_w = grad_gate_w * gain_two
    grad_up_w = grad_up_w * gain_two

    squares = jnp.stack(
        [
            jnp.sum(stream * stream),
            jnp.sum(branch * branch),
            jnp.sum(feed * feed),
            jnp.sum(total_out * total_out),
        ]
    )
    step = 1
    while step < count:
        squares = squares + flip(squares, step)
        step *= 2
    rms_stats = jnp.sqrt(squares / (tokens * count * width))

    def norm_back(gained, values, inverse):
        inner = jnp.sum(gained * values, axis=-1, keepdims=True)
        return inverse * gained - values * (inverse * inverse * inverse) * inner / width

    grad_middle = cot_rows.astype(F32) + norm_back(grad_unit_two, middle, inverse_two)
    grad_branch = gather_seq(grad_middle.astype(BF))

    def reduce_x_z(term, rows):
        parts = term.reshape(columns, 2, rows, -1)
        mine = jnp.where(is_first, parts[:, 0], parts[:, 1])
        theirs = jnp.where(is_first, parts[:, 1], parts[:, 0]).astype(BF)
        summed = (mine + flip(theirs, 4).astype(F32)).astype(BF)
        return scatter_z(summed.reshape(columns * rows, -1))

    part_grad_out = reduce_x_z(contract(attended, grad_branch, 0, 0), rows_small)
    grad_out_w = lax.ppermute(part_grad_out, AXES, [(b, a) for a, b in out_moves]).astype(F32)
    grad_attended = contract(grad_branch, w_out, 1, 1).astype(BF)
    grad_queries, grad_keys, grad_values = attend_back(
        queries, keys_all, values_all, grad_attended.reshape(length, -1, HD), totals
    )
    grad_qkv = jnp.concatenate(
        [
            rotary(grad_queries, positions, -1.0).reshape(length, -1),
            rotary(grad_keys[:, None, :], positions, -1.0)[:, 0],
            grad_values,
        ],
        axis=1,
    ).astype(BF)
    grad_unit_one = scatter_seq(contract(grad_qkv, w_qkv, 1, 1))
    grad_stream = grad_middle + norm_back(grad_unit_one, stream, inverse_one)
    part_grad_qkv = reduce_x_z(contract(unit_one, grad_qkv, 0, 0), seq_size * rows_small)
    back_qkv = lax.all_to_all(
        part_grad_qkv.reshape(seq_size, rows_small, -1), "seq", split_axis=0, concat_axis=1, tiled=True
    )
    back_qkv = back_qkv.reshape(seq_size, rows_small, -1).swapaxes(0, 1).astype(F32)
    grad_attn_gain = jnp.sum(back_qkv * own_qkv, axis=(1, 2))
    back_qkv = back_qkv * gain_one[:, :, None]
    grad_query_w = back_qkv[:, :, :head_cols].reshape(rows_small, -1)
    grad_key_w = back_qkv[:, :, head_cols : head_cols + pair_cols].reshape(rows_small, -1)
    grad_value_w = back_qkv[:, :, head_cols + pair_cols :].reshape(rows_small, -1)
    return (
        total_out.astype(BF)[None],
        grad_stream[None],
        grad_attn_gain,
        grad_query_w,
        grad_key_w,
        grad_value_w,
        grad_out_w,
        grad_ffn_gain,
        grad_gate_w,
        grad_up_w,
        grad_down_w,
        rms_stats,
    )


def solution(mesh):
    token_spec = P("dp", "seq", None)
    gain_spec = P(("dp", "seq"))
    row_spec = P(("dp", "seq"), None)
    ffn_spec = P("dp", "seq")
    weight_specs = (gain_spec, row_spec, row_spec, row_spec, row_spec, gain_spec) + (ffn_spec,) * 3
    return jax.shard_map(
        per_device,
        mesh=mesh,
        in_specs=(token_spec, token_spec) + weight_specs,
        out_specs=(token_spec, token_spec) + weight_specs + (P(),),
        check_vma=False,
    )
```

```python
import functools
import math

import jax
import jax.numpy as jnp
from jax import lax
from jax.experimental import pallas as pl
from jax.experimental.pallas import tpu as pltpu
from jax.sharding import PartitionSpec as P

HD = 64
EPS = 1e-05
AXES = ("dp", "seq")
BF = jnp.bfloat16
F32 = jnp.float32
NEG = -1e30
ROWS = 256
VMEM = 56 << 20


def after(value, *others):
    return lax.optimization_barrier((value,) + others)[0]


def flip(value, mask):
    count = lax.axis_size("dp") * lax.axis_size("seq")
    return lax.ppermute(value, AXES, [(k, k ^ mask) for k in range(count)])


def column_groups():
    size = lax.axis_size("dp")
    return [list(range(start, size, 2)) for start in range(2)]


def gather_z(value):
    return lax.all_gather(value, "dp", axis=1, tiled=True, axis_index_groups=column_groups())


def scatter_z(value):
    return lax.psum_scatter(
        value, "dp", scatter_dimension=1, tiled=True, axis_index_groups=column_groups()
    )


def pick(is_first, own, other):
    return (jnp.where(is_first, own, other), jnp.where(is_first, other, own))


def gather_plane(block):
    half = block.shape[0] // 2
    from_y = flip(block, 2)
    from_x = flip(block, 4)
    top = flip(from_x[:half], 2)
    low = flip(from_y[half:], 4)
    chip = [block, from_y, from_x, top, low]
    return [flip(piece, 1) for piece in chip] + chip


def scatter_plane(theirs, mine, whole=False):
    rows = mine.shape[0] // 4
    half = rows // 2
    part = lambda array, i: array[i * rows : (i + 1) * rows]
    if whole:
        theirs = flip(theirs, 1)
        got = [part(theirs, i) for i in range(4)]
    else:
        got = [flip(part(theirs, i), 1) for i in (3, 0, 1, 2)]
        got = got[1:] + got[:1]
    cross = (part(mine, 3).astype(F32) + got[3].astype(F32)).astype(BF)
    top = flip(cross[:half], 2).astype(F32)
    low = flip(cross[half:], 4).astype(F32)
    if whole:
        mine, theirs = lax.optimization_barrier((mine, theirs, cross))[:2]
        got = [part(theirs, i) for i in range(3)]
    else:
        mine, got = lax.optimization_barrier((mine, got[:3], cross))[:2]
    chip = [part(mine, i).astype(F32) + got[i].astype(F32) for i in range(3)]
    to_x = jnp.concatenate([chip[2][:half] + top, chip[2][half:]], axis=0).astype(BF)
    to_y = jnp.concatenate([chip[1][:half], chip[1][half:] + low], axis=0).astype(BF)
    return chip[0] + flip(to_x, 4).astype(F32) + flip(to_y, 2).astype(F32), cross


def exchange_plane(parts):
    rank = (lax.axis_index("dp") % 2) * 4 + lax.axis_index("seq")
    got = [lax.dynamic_index_in_dim(parts, rank, 0, keepdims=False)]
    for mask in range(1, 8):
        got.append(flip(lax.dynamic_index_in_dim(parts, rank ^ mask, 0, keepdims=False), mask))
    for bit in (1, 2, 4):
        odd = (rank & bit) != 0
        got = [jnp.where(odd, got[k ^ bit], got[k]) for k in range(8)]
    return jnp.stack(got)


def plane_place(sequence, block, rank):
    peer = block ^ rank
    return (1 - peer % 2) * 4 + sequence * 2 + peer // 2


def nt(left, right):
    return lax.dot_general(left, right, (((1,), (1,)), ((), ())), preferred_element_type=F32)


def nn(left, right):
    return lax.dot_general(left, right, (((1,), (0,)), ((), ())), preferred_element_type=F32)


def tn(left, right):
    return lax.dot_general(left, right, (((0,), (0,)), ((), ())), preferred_element_type=F32)


def turn(values, cosine, sine):
    lane = lax.broadcasted_iota(jnp.int32, values.shape, 1)
    partner = jnp.where(lane % HD < HD // 2, pltpu.roll(values, 96, 1), pltpu.roll(values, 32, 1))
    return values * cosine + partner * sine


def twice(values):
    lane = lax.broadcasted_iota(jnp.int32, values.shape, 1)
    swapped = pltpu.roll(values, HD, 1)
    return (jnp.where(lane < HD, values, swapped), jnp.where(lane < HD, swapped, values))


def per_head(values):
    lane = lax.broadcasted_iota(jnp.int32, values.shape, 1)
    zero = jnp.zeros_like(values)
    return jnp.concatenate(
        [jnp.where(lane < HD, values, zero), jnp.where(lane < HD, zero, values)], axis=0
    )


def join_heads(turned):
    back = turned.T
    lane = lax.broadcasted_iota(jnp.int32, (ROWS, 2 * HD), 1)
    return jnp.where(lane < HD, back[:ROWS], back[ROWS:])


def causal(scores):
    place = lax.broadcasted_iota(jnp.int32, scores.shape, 0)
    query = lax.broadcasted_iota(jnp.int32, scores.shape, 1) % ROWS
    return place <= query


def place_rows(ref, place):
    return ref[pl.ds(pl.multiple_of(place * ROWS, ROWS), ROWS), :]


def attend_kernel(rank_ref, q_ref, kv_ref, other_ref, cos_ref, sin_ref, kcos_ref, ksin_ref, out_ref, lse_ref, kk_ref, vt_ref):
    sequence, pair, block = pl.program_id(0), pl.program_id(1), pl.program_id(2)
    blocks = kk_ref.shape[0] // ROWS

    @pl.when((pair == 0) & (block == 0))
    def _():
        for i in range(blocks):
            place = plane_place(sequence, i, rank_ref[0])
            keys = pl.ds(i * ROWS, ROWS)
            rows = place_rows(kv_ref, place) + place_rows(other_ref, (place + 4) % 8)
            kk, vv = twice(turn(rows, kcos_ref[keys, :], ksin_ref[keys, :]))
            kk_ref[keys, :] = kk.astype(BF)
            vt_ref[:, keys] = vv.T.astype(BF)

    both = per_head((turn(q_ref[...], cos_ref[...], sin_ref[...]).astype(BF) * 0.125).astype(BF))

    def rows(count):
        parts = [nt(kk_ref[pl.ds(i * ROWS, ROWS), :], both) for i in range(count)]
        parts[-1] = jnp.where(causal(parts[-1]), parts[-1], NEG)
        highest = functools.reduce(jnp.maximum, [jnp.max(p, axis=0, keepdims=True) for p in parts])
        total = jnp.zeros((1, 2 * ROWS), F32)
        mixed = jnp.zeros((2 * HD, 2 * ROWS), F32)
        for i, part in enumerate(parts):
            weights = jnp.exp(part - highest)
            total = total + jnp.sum(weights, axis=0, keepdims=True)
            mixed = mixed + nn(vt_ref[:, pl.ds(i * ROWS, ROWS)], weights.astype(BF))
        lse_ref[...] = (highest + jnp.log(total)).reshape(lse_ref.shape)
        out_ref[...] = join_heads(mixed / total).astype(BF)

    for count in range(1, blocks + 1):
        pl.when(block == count - 1)(functools.partial(rows, count))


def attention_specs(length, pairs):
    tile = pl.BlockSpec((ROWS, 2 * HD), lambda a, i, j, rank: (plane_place(a, j, rank[0]), i))
    table = pl.BlockSpec((ROWS, 2 * HD), lambda a, i, j, rank: (j, 0))
    whole = pl.BlockSpec((length, 2 * HD), lambda a, i, j, rank: (0, 0))
    both = pl.BlockSpec((2 * length, 2 * HD), lambda a, i, j, rank: (0, 0))
    lse = pl.BlockSpec((1, 1, 1, 1, 2 * ROWS), lambda a, i, j, rank: (a, i, j, 0, 0))
    return (tile, table, whole, both, lse)


def attend(queries, kv, other, tables, rank):
    length = queries.shape[0] // 2
    pairs = queries.shape[1] // (2 * HD)
    blocks = length // ROWS
    tile, table, whole, both, lse = attention_specs(length, pairs)
    return pl.pallas_call(
        attend_kernel,
        name="attend",
        grid_spec=pltpu.PrefetchScalarGridSpec(
            num_scalar_prefetch=1,
            grid=(2, pairs, blocks),
            in_specs=[tile, both, both, table, table, whole, whole],
            out_specs=[tile, lse],
            scratch_shapes=[pltpu.VMEM((length, 2 * HD), BF), pltpu.VMEM((2 * HD, length), BF)],
        ),
        out_shape=[
            jax.ShapeDtypeStruct(queries.shape, BF),
            jax.ShapeDtypeStruct((2, pairs, blocks, 1, 2 * ROWS), F32),
        ],
        compiler_params=pltpu.CompilerParams(vmem_limit_bytes=VMEM),
    )(rank, queries, kv, other, *tables)


def attend_back_kernel(rank_ref, q_ref, kv_ref, other_ref, do_ref, lse_ref, cos_ref, sin_ref, kcos_ref, ksin_ref, dq_ref, dkv_ref, kk_ref, kt_ref, vv_ref, dk_ref, dv_ref):
    sequence, pair, block = pl.program_id(0), pl.program_id(1), pl.program_id(2)
    blocks = kk_ref.shape[0] // ROWS

    @pl.when((pair == 0) & (block == 0))
    def _():
        for i in range(blocks):
            place = plane_place(sequence, i, rank_ref[0])
            keys = pl.ds(i * ROWS, ROWS)
            rows = place_rows(kv_ref, place) + place_rows(other_ref, (place + 4) % 8)
            kk, vv = twice(turn(rows, kcos_ref[keys, :], ksin_ref[keys, :]))
            kk_ref[keys, :] = kk.astype(BF)
            kt_ref[:, keys] = kk.T.astype(BF)
            vv_ref[keys, :] = vv.astype(BF)
        dk_ref[...] = jnp.zeros_like(dk_ref)
        dv_ref[...] = jnp.zeros_like(dv_ref)

    both = per_head((turn(q_ref[...], cos_ref[...], sin_ref[...]).astype(BF) * 0.125).astype(BF))
    grads = per_head(do_ref[...])
    lse = lse_ref[...].reshape(1, 2 * ROWS)

    def rows(count):
        kept = []
        inner = jnp.zeros((1, 2 * ROWS), F32)
        for i in range(count):
            keys = pl.ds(i * ROWS, ROWS)
            weights = jnp.exp(nt(kk_ref[keys, :], both) - lse)
            if i == count - 1:
                weights = jnp.where(causal(weights), weights, 0.0)
            grad_probs = nt(vv_ref[keys, :], grads)
            dv_ref[keys, :] += nn(weights.astype(BF), grads)
            inner = inner + jnp.sum(weights * grad_probs, axis=0, keepdims=True)
            kept.append((weights, grad_probs))
        grad_q = jnp.zeros((2 * HD, 2 * ROWS), F32)
        for i, (weights, grad_probs) in enumerate(kept):
            keys = pl.ds(i * ROWS, ROWS)
            grad_scores = (weights * (grad_probs - inner)).astype(BF)
            dk_ref[keys, :] += nn(grad_scores, both)
            grad_q = grad_q + nn(kt_ref[:, keys], grad_scores)
        dq_ref[...] = turn(join_heads(grad_q) * 0.125, cos_ref[...], -sin_ref[...]).astype(BF)

    for count in range(1, blocks + 1):
        pl.when(block == count - 1)(functools.partial(rows, count))

    @pl.when((pair == pl.num_programs(1) - 1) & (block == blocks - 1))
    def _():
        for i in range(blocks):
            keys = pl.ds(i * ROWS, ROWS)
            dk, dv = dk_ref[keys, :], dv_ref[keys, :]
            lane = lax.broadcasted_iota(jnp.int32, dk.shape, 1)
            joined = jnp.where(lane < HD, dk + pltpu.roll(dk, HD, 1), dv + pltpu.roll(dv, HD, 1))
            place = plane_place(sequence, i, rank_ref[0])
            dkv_ref[pl.ds(pl.multiple_of(place * ROWS, ROWS), ROWS), :] = turn(
                joined, kcos_ref[keys, :], -ksin_ref[keys, :]
            )


def attend_back(queries, kv, other, grad_out, lse_rows, tables, rank):
    length = queries.shape[0] // 2
    pairs = queries.shape[1] // (2 * HD)
    blocks = length // ROWS
    tile, table, whole, both, lse = attention_specs(length, pairs)
    wide = pltpu.VMEM((length, 2 * HD), BF)
    return pl.pallas_call(
        attend_back_kernel,
        name="attend_back",
        grid_spec=pltpu.PrefetchScalarGridSpec(
            num_scalar_prefetch=1,
            grid=(2, pairs, blocks),
            in_specs=[tile, both, both, tile, lse, table, table, whole, whole],
            out_specs=[tile, both],
            scratch_shapes=[wide, pltpu.VMEM((2 * HD, length), BF), wide]
            + [pltpu.VMEM((length, 2 * HD), F32)] * 2,
        ),
        out_shape=[
            jax.ShapeDtypeStruct(queries.shape, BF),
            jax.ShapeDtypeStruct(kv.shape, F32),
        ],
        compiler_params=pltpu.CompilerParams(vmem_limit_bytes=VMEM),
    )(rank, queries, kv, other, grad_out, lse_rows, *tables)


def rotary_tables(length):
    half = HD // 2
    freq = jnp.exp(-math.log(10000.0) * 2.0 * jnp.arange(half, dtype=F32) / HD)
    angles = jnp.arange(length).astype(F32)[:, None] * freq[None, :]
    cosine, sine = jnp.cos(angles), jnp.sin(angles)
    one, zero = jnp.ones((length, HD), F32), jnp.zeros((length, HD), F32)
    return (
        jnp.concatenate([cosine] * 4, axis=1),
        jnp.concatenate([-sine, sine] * 2, axis=1),
        jnp.concatenate([cosine, cosine, one], axis=1),
        jnp.concatenate([-sine, sine, zero], axis=1),
    )


def take_piece(piece_refs, rows_ref):
    step = pl.program_id(0)
    half = rows_ref.shape[0] // 2
    for core in range(2):
        block, from_y, from_x, top, low = piece_refs[5 * core : 5 * core + 5]
        for place, piece in enumerate((block, from_y, from_x)):

            @pl.when(step == 4 * core + place)
            def _(piece=piece):
                rows_ref[...] = piece[...]

        @pl.when(step == 4 * core + 3)
        def _(top=top, low=low):
            rows_ref[:half, :] = top[...]
            rows_ref[half:, :] = low[...]


def resident(array, block=None, place=0):
    shape = array.shape if block is None else block
    return pl.BlockSpec(shape, lambda i: (place, 0), pipeline_mode=pl.Buffered(1))


def row_tile(rows, columns, shift=0):
    return pl.BlockSpec((rows, columns), lambda i: (i + shift, 0))


def call(kernel, name, steps, in_specs, out_specs, out_shape):
    return pl.pallas_call(
        kernel,
        name=name,
        grid=(steps,),
        in_specs=in_specs,
        out_specs=out_specs,
        out_shape=out_shape,
        compiler_params=pltpu.CompilerParams(vmem_limit_bytes=VMEM),
    )


def project_kernel(*refs):
    wq_ref, wkv_ref, rows_ref, q_ref, kv_ref = refs[10:]
    take_piece(refs[:10], rows_ref)
    q_ref[...] = nt(rows_ref[...], wq_ref[...])
    kv_ref[...] = nt(rows_ref[...], wkv_ref[...])


def project(pieces, packed, w_kv):
    tile, width = pieces[0].shape
    columns = 4 * HD
    return call(
        project_kernel,
        "project",
        8,
        [resident(piece) for piece in pieces]
        + [resident(packed, (columns, width)), resident(w_kv)],
        [row_tile(tile, width), row_tile(tile, columns), row_tile(tile, 2 * HD)],
        [
            jax.ShapeDtypeStruct((8 * tile, width), BF),
            jax.ShapeDtypeStruct((8 * tile, columns), F32),
            jax.ShapeDtypeStruct((8 * tile, 2 * HD), F32),
        ],
    )(*pieces, packed, w_kv)


def gathered_dot_kernel(*refs):
    weight_ref, rows_ref, out_ref = refs[10:]
    take_piece(refs[:10], rows_ref)
    out_ref[...] = nt(rows_ref[...], weight_ref[...]).astype(BF)


def gathered_dot(pieces, weight):
    rows, width = pieces[0].shape
    columns = weight.shape[0]
    return call(
        gathered_dot_kernel,
        "gathered_dot",
        8,
        [resident(piece) for piece in pieces] + [resident(weight)],
        [row_tile(rows, width), row_tile(rows, columns)],
        [jax.ShapeDtypeStruct((8 * rows, width), BF), jax.ShapeDtypeStruct((8 * rows, columns), BF)],
    )(*pieces, weight)


def ffn_hidden_kernel(*refs):
    gate_ref, up_ref, rows_ref, hidden_ref, by_gate_ref, by_up_ref = refs[10:]
    take_piece(refs[:10], rows_ref)
    rows = rows_ref[...]
    gate = nt(rows, gate_ref[...])
    up = nt(rows, up_ref[...])
    sigmoid = 1.0 / (1.0 + jnp.exp(-gate))
    silu = gate * sigmoid
    hidden_ref[...] = (silu * up).astype(BF)
    by_gate_ref[...] = (up * sigmoid * (1.0 + gate * (1.0 - sigmoid))).astype(BF)
    by_up_ref[...] = silu.astype(BF)


def ffn_hidden(pieces, w_two):
    rows, width = pieces[0].shape
    columns = w_two.shape[0] // 2
    part = (columns, width)
    return call(
        ffn_hidden_kernel,
        "ffn_hidden",
        8,
        [resident(piece) for piece in pieces] + [resident(w_two, part, 0), resident(w_two, part, 1)],
        [row_tile(rows, width)] + [row_tile(rows, columns)] * 3,
        [jax.ShapeDtypeStruct((8 * rows, width), BF)]
        + [jax.ShapeDtypeStruct((8 * rows, columns), BF)] * 3,
    )(*pieces, w_two, w_two)


def ffn_back_kernel(cot_ref, by_gate_ref, by_up_ref, down_ref, gate_ref, up_ref, gg_ref, gu_ref, part_ref):
    grad_hidden = nt(cot_ref[...], down_ref[...])
    grad_gate = (grad_hidden * by_gate_ref[...].astype(F32)).astype(BF)
    grad_up = (grad_hidden * by_up_ref[...].astype(F32)).astype(BF)
    gg_ref[...] = grad_gate
    gu_ref[...] = grad_up
    part_ref[...] = (nn(grad_gate, gate_ref[...]) + nn(grad_up, up_ref[...])).astype(BF)


def ffn_back(cot, by_gate, by_up, w_down, w_two, which):
    rows, width = cot.shape[0] // 8, cot.shape[1]
    columns = w_down.shape[0]
    part = (columns, width)
    return call(
        ffn_back_kernel,
        "ffn_back",
        4,
        [row_tile(rows, width, 4 * which)]
        + [row_tile(rows, columns, 4 * which)] * 2
        + [resident(w_down), resident(w_two, part, 0), resident(w_two, part, 1)],
        [row_tile(rows, columns)] * 2 + [row_tile(rows, width)],
        [jax.ShapeDtypeStruct((4 * rows, columns), BF)] * 2
        + [jax.ShapeDtypeStruct((4 * rows, width), BF)],
    )(cot, by_gate, by_up, w_down, w_two, w_two)


def weight_grad_kernel(rows_ref, *refs, parts):
    out_ref = refs[-1]
    place = 0
    for start in range(0, len(refs) - 1, parts):
        total = 0.0
        row = 0
        for grad_ref in refs[start : start + parts]:
            count = grad_ref.shape[0]
            total = total + tn(rows_ref[row : row + count, :], grad_ref[...])
            row += count
        columns = total.shape[1]
        out_ref[place : place + columns, :] = total.T.astype(BF)
        place += columns


def weight_grad(rows, *grads):
    count, width = rows.shape
    tile = width // 4
    columns = sum(grad[0].shape[1] for grad in grads)
    flat = [part for grad in grads for part in grad]
    return call(
        functools.partial(weight_grad_kernel, parts=len(grads[0])),
        "weight_grad",
        4,
        [pl.BlockSpec((count, tile), lambda i: (0, i))] + [resident(part) for part in flat],
        pl.BlockSpec((columns, tile), lambda i: (0, i)),
        jax.ShapeDtypeStruct((columns, width), BF),
    )(rows, *flat)


def out_grad_kernel(rows_ref, grad_ref, out_ref, *, small):
    product = tn(rows_ref[...], grad_ref[...]).astype(BF)
    tile = product.shape[1]
    for group in range(product.shape[0] // small):
        out_ref[:, group * tile : (group + 1) * tile] = product[group * small : (group + 1) * small]


def out_grad(rows, grad, small, pieces):
    count, columns = rows.shape
    width = grad.shape[1]
    tile = width // pieces
    return call(
        functools.partial(out_grad_kernel, small=small),
        "out_grad",
        pieces,
        [resident(rows), pl.BlockSpec((count, tile), lambda i: (0, i))],
        row_tile(small, columns // small * tile),
        jax.ShapeDtypeStruct((pieces * small, columns // small * tile), BF),
    )(rows, grad)


def per_device(
    residual,
    cotangent,
    attn_gain,
    query_weight,
    key_weight,
    value_weight,
    out_weight,
    ffn_gain,
    gate_weight,
    up_weight,
    down_weight,
):
    dp_size = lax.axis_size("dp")
    seq_size = lax.axis_size("seq")
    count = dp_size * seq_size
    planes = dp_size // 2
    rank = lax.axis_index("seq")
    is_first = lax.axis_index("dp") % 2 == 0
    first_core = rank % 2 == 0
    place = jnp.full((1,), rank, jnp.int32)
    tokens = residual.shape[1]
    width = residual.shape[2]
    small = query_weight.shape[0]
    rows_ffn = gate_weight.shape[0]
    head_cols = query_weight.shape[1] // 8
    hidden_half = gate_weight.shape[1] // 2

    out_moves = [(k, (k % planes) * 8 + k // planes) for k in range(count)]
    plane_out = lax.ppermute(out_weight, AXES, out_moves)

    gain_one = attn_gain.astype(F32)[:, None, None]
    own_q = query_weight.reshape(small, 8, head_cols).astype(F32)
    own_kv = jnp.stack(
        [key_weight.reshape(small, 4, HD), value_weight.reshape(small, 4, HD)], axis=2
    ).reshape(small, 8, HD).astype(F32)
    send = (jnp.concatenate([own_q, own_kv], axis=2) * gain_one).astype(BF).swapaxes(0, 1)
    plane_qkv = exchange_plane(send).reshape(8 * small, -1).T
    pieces = width // (8 * small)

    def pack_out(rows, groups):
        blocks = rows.reshape(groups, small, pieces, 8 * small)
        return blocks.transpose(2, 1, 0, 3).reshape(pieces * small, -1)

    def unpack_out(rows, groups):
        blocks = rows.reshape(pieces, small, groups, 8 * small)
        return blocks.transpose(2, 1, 0, 3).reshape(groups * small, -1)

    own_packed = jnp.concatenate(
        [plane_qkv[:head_cols], pack_out(plane_out, 1), plane_qkv[head_cols:]], axis=0
    )
    slots = jnp.zeros((seq_size, small), F32)
    slots = lax.dynamic_update_index_in_dim(slots, ffn_gain.astype(F32), rank, 0)
    slots = slots + flip(slots, 1)
    slots = slots + flip(slots, 2)
    gain_two = slots.reshape(rows_ffn)
    own_packed, gain_two = lax.optimization_barrier((own_packed, gain_two))
    packed = gather_z(own_packed)

    def halves(weights):
        parts = [(w[:hidden_half], w[hidden_half:]) for w in weights]
        mine = jnp.concatenate([jnp.where(is_first, left, right) for left, right in parts], axis=0)
        theirs = jnp.concatenate([jnp.where(is_first, right, left) for left, right in parts], axis=0)
        return jnp.concatenate(pick(is_first, mine, flip(theirs, 4)), axis=1)

    def scaled(weight):
        return (weight.T.astype(F32) * gain_two).astype(BF)

    stream = residual[0].astype(F32)
    inverse_one = lax.rsqrt(jnp.mean(stream * stream, axis=-1, keepdims=True) + EPS)
    unit_one = gather_plane((stream * inverse_one).astype(BF))
    gate_late, up_late = lax.optimization_barrier((gate_weight, up_weight, *unit_one[6:8]))[:2]
    half_two = halves([scaled(gate_late), scaled(up_late)])
    half_down = halves([after(down_weight, *unit_one[8:]).T])
    w_two = gather_z(half_two)
    w_down = gather_z(half_down)
    cot_rows = cotangent[0]
    cot_early = after(cot_rows, *unit_one[8:])
    cot_chip = [cot_early, flip(cot_early, 2), flip(cot_early, 4), flip(cot_early, 6)]
    tables = rotary_tables(tokens * seq_size)
    packed, unit_one, half_down, tables = lax.optimization_barrier(
        (packed, unit_one, half_down, tables)
    )

    w_out = unpack_out(packed[head_cols : 2 * head_cols], planes)
    own_half = packed[2 * head_cols :]
    nothing = jnp.zeros_like(own_half)
    w_kv = jnp.concatenate(
        [jnp.where(first_core, own_half, nothing), jnp.where(first_core, nothing, own_half)], axis=0
    )
    unit_one, queries, kv = project(unit_one, packed, w_kv)
    kv_other = flip(kv, 1)
    attended, lse = attend(queries, kv, kv_other, tables, place)
    attended, *cot_chip = lax.optimization_barrier((attended, *cot_chip))
    part_rows = attended.shape[0] // 2
    branch, crossed = scatter_plane(
        nn(attended[:part_rows], w_out).astype(BF), nn(attended[part_rows:], w_out).astype(BF)
    )
    middle = stream + branch
    cot_chip = [after(cot_chip[0], crossed)] + cot_chip[1:]
    cot_all = jnp.concatenate([flip(piece, 1) for piece in cot_chip] + cot_chip, axis=0)
    middle, cot_all = lax.optimization_barrier((middle, cot_all))
    inverse_two = lax.rsqrt(jnp.mean(middle * middle, axis=-1, keepdims=True) + EPS)

    unit_two, hidden, by_gate, by_up = ffn_hidden(
        gather_plane((middle * inverse_two).astype(BF)), w_two
    )
    term_down = weight_grad(cot_all, [hidden])
    sum_down = scatter_z(term_down)
    by_gate = after(by_gate, term_down)
    grad_gate_a, grad_up_a, theirs = ffn_back(cot_all, by_gate, by_up, w_down, w_two, 0)
    grad_gate_b, grad_up_b, mine = ffn_back(cot_all, by_gate, by_up, w_down, w_two, 1)
    grad_unit_two, crossed = scatter_plane(theirs, mine, True)
    unit_two = after(unit_two, crossed)
    term_two = weight_grad(unit_two, [grad_gate_a, grad_gate_b], [grad_up_a, grad_up_b])
    grad_unit_two, sum_down = lax.optimization_barrier((grad_unit_two, sum_down, term_two))[:2]
    sum_two = scatter_z(term_two)

    def own_rows(term):
        first, second = term[:, :rows_ffn], term[:, rows_ffn:]
        other = flip(jnp.where(is_first, second, first), 4)
        return pick(is_first, jnp.where(is_first, first, second), other)

    grad_down_w = jnp.concatenate(own_rows(sum_down), axis=0).T.astype(F32)
    two_first, two_second = own_rows(sum_two)
    grad_gate_w = jnp.concatenate([two_first[:hidden_half], two_second[:hidden_half]], axis=0).T
    grad_up_w = jnp.concatenate([two_first[hidden_half:], two_second[hidden_half:]], axis=0).T
    grad_gate_w, grad_up_w = grad_gate_w.astype(F32), grad_up_w.astype(F32)
    gain_rows = jnp.sum(
        grad_gate_w * gate_weight.astype(F32) + grad_up_w * up_weight.astype(F32), axis=1
    )
    gain_rows = gain_rows + flip(gain_rows, 1)
    gain_rows = gain_rows + flip(gain_rows, 2)
    grad_ffn_gain = lax.dynamic_slice_in_dim(gain_rows, rank * small, small)
    grad_gate_w = grad_gate_w * gain_two[:, None]
    grad_up_w = grad_up_w * gain_two[:, None]

    def norm_back(gained, values, inverse):
        inner = jnp.sum(gained * values, axis=-1, keepdims=True)
        return inverse * gained - values * (inverse * inverse * inverse) * inner / width

    grad_middle = cot_rows.astype(F32) + norm_back(grad_unit_two, middle, inverse_two)
    grad_branch = gather_plane(grad_middle.astype(BF))

    hidden_late = after(hidden, grad_middle)
    feed, crossed = scatter_plane(
        nn(hidden_late[:part_rows], w_down).astype(BF), nn(hidden_late[part_rows:], w_down).astype(BF)
    )
    total_out = middle + feed
    squares = jnp.stack(
        [
            jnp.sum(stream * stream),
            jnp.sum(branch * branch),
            jnp.sum(feed * feed),
            jnp.sum(total_out * total_out),
        ]
    )
    step = 1
    while step < count:
        squares = squares + flip(squares, step)
        step *= 2
    rms_stats = jnp.sqrt(squares / (tokens * count * width))

    w_out = after(w_out, crossed)
    grad_branch, grad_attended = gathered_dot(grad_branch, w_out)
    term_out = out_grad(attended, grad_branch, small, pieces)
    grad_attended = after(grad_attended, term_out)
    grad_q, grad_kv = attend_back(queries, kv, kv_other, grad_attended, lse, tables, place)
    kv_back = flip(grad_kv, 1)
    kv_back = jnp.concatenate([kv_back[part_rows:], kv_back[:part_rows]], axis=0)
    grad_kv = (grad_kv + kv_back).astype(BF)
    term_qkv = weight_grad(unit_one, [grad_q], [grad_kv])
    term_kv = jnp.where(first_core, term_qkv[head_cols : head_cols + HD], term_qkv[head_cols + HD :])
    term_qkv = jnp.concatenate([term_qkv[:head_cols], term_out, term_kv], axis=0)
    sums = scatter_z(after(term_qkv, sum_two))
    late_q, late_kv = lax.optimization_barrier((grad_q, grad_kv, term_qkv))[:2]
    late = jnp.concatenate([late_q, late_kv], axis=1)
    w_qkv = jnp.concatenate([packed[:head_cols], w_kv], axis=0)
    grad_unit_one, crossed = scatter_plane(
        nn(late[:part_rows], w_qkv).astype(BF), nn(late[part_rows:], w_qkv).astype(BF)
    )
    grad_stream = grad_middle + norm_back(grad_unit_one, stream, inverse_one)
    others = (grad_stream, total_out, rms_stats, grad_down_w, grad_gate_w, grad_up_w, grad_ffn_gain)
    sums, others = lax.optimization_barrier((sums, others))
    grad_stream, total_out, rms_stats, grad_down_w, grad_gate_w, grad_up_w, grad_ffn_gain = others
    grad_out_rows = unpack_out(sums[head_cols : 2 * head_cols], 1)
    grad_out_w = lax.ppermute(grad_out_rows, AXES, [(b, a) for a, b in out_moves]).astype(F32)
    plane_grad = jnp.concatenate([sums[:head_cols], sums[2 * head_cols :]], axis=0).T
    back = exchange_plane(plane_grad.reshape(8, small, -1)).swapaxes(0, 1).astype(F32)
    back_q, back_kv = back[:, :, :head_cols], back[:, :, head_cols:]
    grad_attn_gain = jnp.sum(back_q * own_q, axis=(1, 2)) + jnp.sum(back_kv * own_kv, axis=(1, 2))
    back_kv = (back_kv * gain_one).reshape(small, 4, 2, HD)
    return (
        total_out.astype(BF)[None],
        grad_stream[None],
        grad_attn_gain,
        (back_q * gain_one).reshape(small, -1),
        back_kv[:, :, 0].reshape(small, -1),
        back_kv[:, :, 1].reshape(small, -1),
        grad_out_w,
        grad_ffn_gain,
        grad_gate_w,
        grad_up_w,
        grad_down_w,
        rms_stats,
    )


def solution(mesh):
    token_spec = P("dp", "seq", None)
    gain_spec = P(("dp", "seq"))
    row_spec = P(("dp", "seq"), None)
    ffn_spec = P("dp", "seq")
    weight_specs = (gain_spec, row_spec, row_spec, row_spec, row_spec, gain_spec) + (ffn_spec,) * 3
    return jax.shard_map(
        per_device,
        mesh=mesh,
        in_specs=(token_spec, token_spec) + weight_specs,
        out_specs=(token_spec, token_spec) + weight_specs + (P(),),
        check_vma=False,
    )
```

```python
import functools
import math

import jax
import jax.numpy as jnp
from jax import lax
from jax.experimental import pallas as pl
from jax.experimental.pallas import tpu as pltpu
from jax.sharding import PartitionSpec as P

HD = 64
EPS = 1e-05
AXES = ("dp", "seq")
BF = jnp.bfloat16
F32 = jnp.float32
NEG = -1e30
ROWS = 256
VMEM = 56 << 20
EXTRA = 16


def after(value, *others):
    return lax.optimization_barrier((value,) + others)[0]


def flip(value, mask):
    count = lax.axis_size("dp") * lax.axis_size("seq")
    return lax.ppermute(value, AXES, [(k, k ^ mask) for k in range(count)])


def column_groups():
    size = lax.axis_size("dp")
    return [list(range(start, size, 2)) for start in range(2)]


def gather_z(value):
    return lax.all_gather(value, "dp", axis=1, tiled=True, axis_index_groups=column_groups())


def scatter_z(value):
    return lax.psum_scatter(
        value, "dp", scatter_dimension=1, tiled=True, axis_index_groups=column_groups()
    )


def pick(is_first, own, other):
    return (jnp.where(is_first, own, other), jnp.where(is_first, other, own))


def gather_plane(block):
    half = block.shape[0] // 2
    from_y = flip(block, 2)
    from_x = flip(block, 4)
    top = flip(from_x[:half], 2)
    low = flip(from_y[half:], 4)
    chip = [block, from_y, from_x, top, low]
    return [flip(piece, 1) for piece in chip] + chip


def scatter_start(theirs, mine, whole=False):
    rows = mine.shape[0] // 4
    half = rows // 2
    part = lambda array, i: array[i * rows : (i + 1) * rows]
    if whole:
        theirs = flip(theirs, 1)
        got = [part(theirs, i) for i in range(4)]
    else:
        got = [flip(part(theirs, i), 1) for i in (3, 0, 1, 2)]
        got = got[1:] + got[:1]
    cross = (part(mine, 3).astype(F32) + got[3].astype(F32)).astype(BF)
    relayed = (flip(cross[:half], 2), flip(cross[half:], 4))
    if whole:
        mine, theirs = lax.optimization_barrier((mine, theirs, cross))[:2]
        got = [part(theirs, i) for i in range(3)]
    else:
        mine, got = lax.optimization_barrier((mine, got[:3], cross))[:2]
    chip = [part(mine, i).astype(F32) + got[i].astype(F32) for i in range(3)]
    return (chip, relayed, cross)


def scatter_middle(state):
    (_, to_y, to_x), (top, low), _ = state
    half = top.shape[0]
    to_x = jnp.concatenate([to_x[:half] + top.astype(F32), to_x[half:]], axis=0).astype(BF)
    to_y = jnp.concatenate([to_y[:half], to_y[half:] + low.astype(F32)], axis=0).astype(BF)
    return (to_x, to_y)


def scatter_end(state, sent):
    return (flip(sent[0], 4), flip(sent[1], 2))


def scatter_sum(state, received):
    return state[0][0] + received[0].astype(F32) + received[1].astype(F32)


def exchange_plane(parts):
    rank = (lax.axis_index("dp") % 2) * 4 + lax.axis_index("seq")
    got = [lax.dynamic_index_in_dim(parts, rank, 0, keepdims=False)]
    for mask in range(1, 8):
        got.append(flip(lax.dynamic_index_in_dim(parts, rank ^ mask, 0, keepdims=False), mask))
    for bit in (1, 2, 4):
        odd = (rank & bit) != 0
        got = [jnp.where(odd, got[k ^ bit], got[k]) for k in range(8)]
    return jnp.stack(got)


def plane_place(sequence, block, rank):
    peer = block ^ rank
    return (1 - peer % 2) * 4 + sequence * 2 + peer // 2


def nt(left, right):
    return lax.dot_general(left, right, (((1,), (1,)), ((), ())), preferred_element_type=F32)


def nn(left, right):
    return lax.dot_general(left, right, (((1,), (0,)), ((), ())), preferred_element_type=F32)


def tn(left, right):
    return lax.dot_general(left, right, (((0,), (0,)), ((), ())), preferred_element_type=F32)


def turn(values, cosine, sine):
    lane = lax.broadcasted_iota(jnp.int32, values.shape, 1)
    partner = jnp.where(lane % HD < HD // 2, pltpu.roll(values, 96, 1), pltpu.roll(values, 32, 1))
    return values * cosine + partner * sine


def twice(values):
    lane = lax.broadcasted_iota(jnp.int32, values.shape, 1)
    swapped = pltpu.roll(values, HD, 1)
    return (jnp.where(lane < HD, values, swapped), jnp.where(lane < HD, swapped, values))


def per_head(values):
    lane = lax.broadcasted_iota(jnp.int32, values.shape, 1)
    zero = jnp.zeros_like(values)
    return jnp.concatenate(
        [jnp.where(lane < HD, values, zero), jnp.where(lane < HD, zero, values)], axis=0
    )


def join_heads(turned):
    back = turned.T
    lane = lax.broadcasted_iota(jnp.int32, (ROWS, 2 * HD), 1)
    return jnp.where(lane < HD, back[:ROWS], back[ROWS:])


def causal(scores):
    place = lax.broadcasted_iota(jnp.int32, scores.shape, 0)
    query = lax.broadcasted_iota(jnp.int32, scores.shape, 1) % ROWS
    return place <= query


def place_rows(ref, place):
    return ref[pl.ds(pl.multiple_of(place * ROWS, ROWS), ROWS), :]


def attend_kernel(rank_ref, q_ref, kv_ref, other_ref, cos_ref, sin_ref, kcos_ref, ksin_ref, out_ref, lse_ref, kk_ref, vt_ref):
    sequence, pair, block = pl.program_id(0), pl.program_id(1), pl.program_id(2)
    blocks = kk_ref.shape[0] // ROWS

    @pl.when((pair == 0) & (block == 0))
    def _():
        for i in range(blocks):
            place = plane_place(sequence, i, rank_ref[0])
            keys = pl.ds(i * ROWS, ROWS)
            rows = place_rows(kv_ref, place) + place_rows(other_ref, (place + 4) % 8)
            kk, vv = twice(turn(rows, kcos_ref[keys, :], ksin_ref[keys, :]))
            kk_ref[keys, :] = kk.astype(BF)
            vt_ref[:, keys] = vv.T.astype(BF)

    both = per_head((turn(q_ref[...], cos_ref[...], sin_ref[...]).astype(BF) * 0.125).astype(BF))

    def rows(count):
        parts = [nt(kk_ref[pl.ds(i * ROWS, ROWS), :], both) for i in range(count)]
        parts[-1] = jnp.where(causal(parts[-1]), parts[-1], NEG)
        highest = functools.reduce(jnp.maximum, [jnp.max(p, axis=0, keepdims=True) for p in parts])
        total = jnp.zeros((1, 2 * ROWS), F32)
        mixed = jnp.zeros((2 * HD, 2 * ROWS), F32)
        for i, part in enumerate(parts):
            weights = jnp.exp(part - highest)
            total = total + jnp.sum(weights, axis=0, keepdims=True)
            mixed = mixed + nn(vt_ref[:, pl.ds(i * ROWS, ROWS)], weights.astype(BF))
        lse_ref[...] = (highest + jnp.log(total)).reshape(lse_ref.shape)
        out_ref[...] = join_heads(mixed / total).astype(BF)

    for count in range(1, blocks + 1):
        pl.when(block == count - 1)(functools.partial(rows, count))


def attention_specs(length, pairs):
    tile = pl.BlockSpec((ROWS, 2 * HD), lambda a, i, j, rank: (plane_place(a, j, rank[0]), i))
    table = pl.BlockSpec((ROWS, 2 * HD), lambda a, i, j, rank: (j, 0))
    whole = pl.BlockSpec((length, 2 * HD), lambda a, i, j, rank: (0, 0))
    both = pl.BlockSpec((2 * length, 2 * HD), lambda a, i, j, rank: (0, 0))
    lse = pl.BlockSpec((1, 1, 1, 1, 2 * ROWS), lambda a, i, j, rank: (a, i, j, 0, 0))
    return (tile, table, whole, both, lse)


def attend(queries, kv, other, tables, rank):
    length = queries.shape[0] // 2
    pairs = queries.shape[1] // (2 * HD)
    blocks = length // ROWS
    tile, table, whole, both, lse = attention_specs(length, pairs)
    return pl.pallas_call(
        attend_kernel,
        name="attend",
        grid_spec=pltpu.PrefetchScalarGridSpec(
            num_scalar_prefetch=1,
            grid=(2, pairs, blocks),
            in_specs=[tile, both, both, table, table, whole, whole],
            out_specs=[tile, lse],
            scratch_shapes=[pltpu.VMEM((length, 2 * HD), BF), pltpu.VMEM((2 * HD, length), BF)],
        ),
        out_shape=[
            jax.ShapeDtypeStruct(queries.shape, BF),
            jax.ShapeDtypeStruct((2, pairs, blocks, 1, 2 * ROWS), F32),
        ],
        compiler_params=pltpu.CompilerParams(vmem_limit_bytes=VMEM),
        cost_estimate=cost(16 * pairs * length * length * HD * 4),
    )(rank, queries, kv, other, *tables)


def attend_back_kernel(rank_ref, q_ref, kv_ref, other_ref, do_ref, lse_ref, cos_ref, sin_ref, kcos_ref, ksin_ref, dq_ref, dkv_ref, kk_ref, kt_ref, vv_ref, dk_ref, dv_ref):
    sequence, pair, block = pl.program_id(0), pl.program_id(1), pl.program_id(2)
    blocks = kk_ref.shape[0] // ROWS

    @pl.when((pair == 0) & (block == 0))
    def _():
        for i in range(blocks):
            place = plane_place(sequence, i, rank_ref[0])
            keys = pl.ds(i * ROWS, ROWS)
            rows = place_rows(kv_ref, place) + place_rows(other_ref, (place + 4) % 8)
            kk, vv = twice(turn(rows, kcos_ref[keys, :], ksin_ref[keys, :]))
            kk_ref[keys, :] = kk.astype(BF)
            kt_ref[:, keys] = kk.T.astype(BF)
            vv_ref[keys, :] = vv.astype(BF)
        dk_ref[...] = jnp.zeros_like(dk_ref)
        dv_ref[...] = jnp.zeros_like(dv_ref)

    both = per_head((turn(q_ref[...], cos_ref[...], sin_ref[...]).astype(BF) * 0.125).astype(BF))
    grads = per_head(do_ref[...])
    lse = lse_ref[...].reshape(1, 2 * ROWS)

    def rows(count):
        kept = []
        inner = jnp.zeros((1, 2 * ROWS), F32)
        for i in range(count):
            keys = pl.ds(i * ROWS, ROWS)
            weights = jnp.exp(nt(kk_ref[keys, :], both) - lse)
            if i == count - 1:
                weights = jnp.where(causal(weights), weights, 0.0)
            grad_probs = nt(vv_ref[keys, :], grads)
            dv_ref[keys, :] += nn(weights.astype(BF), grads)
            inner = inner + jnp.sum(weights * grad_probs, axis=0, keepdims=True)
            kept.append((weights, grad_probs))
        grad_q = jnp.zeros((2 * HD, 2 * ROWS), F32)
        for i, (weights, grad_probs) in enumerate(kept):
            keys = pl.ds(i * ROWS, ROWS)
            grad_scores = (weights * (grad_probs - inner)).astype(BF)
            dk_ref[keys, :] += nn(grad_scores, both)
            grad_q = grad_q + nn(kt_ref[:, keys], grad_scores)
        dq_ref[...] = turn(join_heads(grad_q) * 0.125, cos_ref[...], -sin_ref[...]).astype(BF)

    for count in range(1, blocks + 1):
        pl.when(block == count - 1)(functools.partial(rows, count))

    @pl.when((pair == pl.num_programs(1) - 1) & (block == blocks - 1))
    def _():
        for i in range(blocks):
            keys = pl.ds(i * ROWS, ROWS)
            dk, dv = dk_ref[keys, :], dv_ref[keys, :]
            lane = lax.broadcasted_iota(jnp.int32, dk.shape, 1)
            joined = jnp.where(lane < HD, dk + pltpu.roll(dk, HD, 1), dv + pltpu.roll(dv, HD, 1))
            place = plane_place(sequence, i, rank_ref[0])
            dkv_ref[pl.ds(pl.multiple_of(place * ROWS, ROWS), ROWS), :] = turn(
                joined, kcos_ref[keys, :], -ksin_ref[keys, :]
            )


def attend_back(queries, kv, other, grad_out, lse_rows, tables, rank):
    length = queries.shape[0] // 2
    pairs = queries.shape[1] // (2 * HD)
    blocks = length // ROWS
    tile, table, whole, both, lse = attention_specs(length, pairs)
    wide = pltpu.VMEM((length, 2 * HD), BF)
    return pl.pallas_call(
        attend_back_kernel,
        name="attend_back",
        grid_spec=pltpu.PrefetchScalarGridSpec(
            num_scalar_prefetch=1,
            grid=(2, pairs, blocks),
            in_specs=[tile, both, both, tile, lse, table, table, whole, whole],
            out_specs=[tile, both],
            scratch_shapes=[wide, pltpu.VMEM((2 * HD, length), BF), wide]
            + [pltpu.VMEM((length, 2 * HD), F32)] * 2,
        ),
        out_shape=[
            jax.ShapeDtypeStruct(queries.shape, BF),
            jax.ShapeDtypeStruct(kv.shape, F32),
        ],
        compiler_params=pltpu.CompilerParams(vmem_limit_bytes=VMEM),
        cost_estimate=cost(28 * pairs * length * length * HD * 4),
    )(rank, queries, kv, other, grad_out, lse_rows, *tables)


def rotary_tables(length):
    half = HD // 2
    freq = jnp.exp(-math.log(10000.0) * 2.0 * jnp.arange(half, dtype=F32) / HD)
    angles = jnp.arange(length).astype(F32)[:, None] * freq[None, :]
    cosine, sine = jnp.cos(angles), jnp.sin(angles)
    one, zero = jnp.ones((length, HD), F32), jnp.zeros((length, HD), F32)
    return (
        jnp.concatenate([cosine] * 4, axis=1),
        jnp.concatenate([-sine, sine] * 2, axis=1),
        jnp.concatenate([cosine, cosine, one], axis=1),
        jnp.concatenate([-sine, sine, zero], axis=1),
    )


def take_piece(piece_refs, rows_ref):
    step = pl.program_id(0)
    half = rows_ref.shape[0] // 2
    for core in range(2):
        block, from_y, from_x, top, low = piece_refs[5 * core : 5 * core + 5]
        for place, piece in enumerate((block, from_y, from_x)):

            @pl.when(step == 4 * core + place)
            def _(piece=piece):
                rows_ref[...] = piece[...]

        @pl.when(step == 4 * core + 3)
        def _(top=top, low=low):
            rows_ref[:half, :] = top[...]
            rows_ref[half:, :] = low[...]


def resident(array, block=None, place=0):
    shape = array.shape if block is None else block
    return pl.BlockSpec(shape, lambda i: (place, 0), pipeline_mode=pl.Buffered(1))


def row_tile(rows, columns, shift=0):
    return pl.BlockSpec((rows, columns), lambda i: (i + shift, 0))


def cost(flops, transcendentals=0):
    return pl.CostEstimate(flops=flops, transcendentals=transcendentals, bytes_accessed=flops // 300)


def call(kernel, name, steps, in_specs, out_specs, out_shape, flops, scratch_shapes=()):
    return pl.pallas_call(
        kernel,
        name=name,
        grid=(steps,),
        in_specs=in_specs,
        out_specs=out_specs,
        out_shape=out_shape,
        scratch_shapes=scratch_shapes,
        cost_estimate=cost(flops),
        compiler_params=pltpu.CompilerParams(vmem_limit_bytes=VMEM),
    )


def project_kernel(*refs):
    gain_ref, wq_ref, wkv_ref, rows_ref, q_ref, kv_ref, raw_ref = refs[10:]
    take_piece(refs[:10], raw_ref)
    rows = raw_ref[...].astype(F32)
    inverse = lax.rsqrt(jnp.mean(rows * rows, axis=-1, keepdims=True) + EPS)
    rows = (rows * inverse * gain_ref[...]).astype(BF)
    rows_ref[...] = rows
    q_ref[...] = nt(rows, wq_ref[...])
    kv_ref[...] = nt(rows, wkv_ref[...])


def project(pieces, gain, packed, w_kv):
    tile, width = pieces[0].shape
    columns = 4 * HD
    return call(
        project_kernel,
        "project",
        8,
        [resident(piece) for piece in pieces]
        + [resident(gain), resident(packed, (columns, width)), resident(w_kv)],
        [row_tile(tile, width), row_tile(tile, columns), row_tile(tile, 2 * HD)],
        [
            jax.ShapeDtypeStruct((8 * tile, width), BF),
            jax.ShapeDtypeStruct((8 * tile, columns), F32),
            jax.ShapeDtypeStruct((8 * tile, 2 * HD), F32),
        ],
        16 * tile * width * 8 * HD,
        [pltpu.VMEM((tile, width), BF)],
    )(*pieces, gain, packed, w_kv)


def gathered_dot_kernel(*refs):
    weight_ref, rows_ref, out_ref = refs[10:]
    take_piece(refs[:10], rows_ref)
    out_ref[...] = nt(rows_ref[...], weight_ref[...]).astype(BF)


def gathered_dot(pieces, weight):
    rows, width = pieces[0].shape
    columns = weight.shape[0]
    return call(
        gathered_dot_kernel,
        "gathered_dot",
        8,
        [resident(piece) for piece in pieces] + [resident(weight)],
        [row_tile(rows, width), row_tile(rows, columns)],
        [jax.ShapeDtypeStruct((8 * rows, width), BF), jax.ShapeDtypeStruct((8 * rows, columns), BF)],
        32 * rows * width * columns,
    )(*pieces, weight)


def ffn_hidden_kernel(*refs):
    gate_ref, up_ref, rows_ref, hidden_ref, by_gate_ref, by_up_ref = refs[10:]
    take_piece(refs[:10], rows_ref)
    rows = rows_ref[...]
    gate = nt(rows, gate_ref[...])
    up = nt(rows, up_ref[...])
    sigmoid = 1.0 / (1.0 + jnp.exp(-gate))
    silu = gate * sigmoid
    hidden_ref[...] = (silu * up).astype(BF)
    by_gate_ref[...] = (up * sigmoid * (1.0 + gate * (1.0 - sigmoid))).astype(BF)
    by_up_ref[...] = silu.astype(BF)


def ffn_hidden(pieces, w_two):
    rows, width = pieces[0].shape
    columns = w_two.shape[0] // 2
    part = (columns, width)
    return call(
        ffn_hidden_kernel,
        "ffn_hidden",
        8,
        [resident(piece) for piece in pieces] + [resident(w_two, part, 0), resident(w_two, part, 1)],
        [row_tile(rows, width)] + [row_tile(rows, columns)] * 3,
        [jax.ShapeDtypeStruct((8 * rows, width), BF)]
        + [jax.ShapeDtypeStruct((8 * rows, columns), BF)] * 3,
        32 * rows * width * columns,
    )(*pieces, w_two, w_two)


def ffn_back_kernel(cot_ref, by_gate_ref, by_up_ref, down_ref, gate_ref, up_ref, gg_ref, gu_ref, part_ref):
    grad_hidden = nt(cot_ref[...], down_ref[...])
    grad_gate = (grad_hidden * by_gate_ref[...].astype(F32)).astype(BF)
    grad_up = (grad_hidden * by_up_ref[...].astype(F32)).astype(BF)
    gg_ref[...] = grad_gate
    gu_ref[...] = grad_up
    part_ref[...] = (nn(grad_gate, gate_ref[...]) + nn(grad_up, up_ref[...])).astype(BF)


def ffn_back(cot, by_gate, by_up, w_down, w_two, which):
    rows, width = cot.shape[0] // 8, cot.shape[1]
    columns = w_down.shape[0]
    part = (columns, width)
    return call(
        ffn_back_kernel,
        "ffn_back",
        4,
        [row_tile(rows, width, 4 * which)]
        + [row_tile(rows, columns, 4 * which)] * 2
        + [resident(w_down), resident(w_two, part, 0), resident(w_two, part, 1)],
        [row_tile(rows, columns)] * 2 + [row_tile(rows, width)],
        [jax.ShapeDtypeStruct((4 * rows, columns), BF)] * 2
        + [jax.ShapeDtypeStruct((4 * rows, width), BF)],
        24 * rows * width * columns,
    )(cot, by_gate, by_up, w_down, w_two, w_two)


def weight_grad_kernel(rows_ref, *refs, parts, summed):
    out_ref = refs[-1]
    width = parts + 1 if summed else parts
    place = 0
    row_sum = 0.0
    for start in range(0, len(refs) - 1, width):
        total = 0.0
        row = 0
        for grad_ref in refs[start : start + parts]:
            count = grad_ref.shape[0]
            total = total + tn(rows_ref[row : row + count, :], grad_ref[...])
            row += count
        total = total.T
        columns = total.shape[0]
        if summed:
            row_sum = row_sum + jnp.sum(total * refs[start + parts][...].astype(F32), axis=0, keepdims=True)
        out_ref[place : place + columns, :] = total.astype(BF)
        place += columns
    if summed:
        high = row_sum.astype(BF).astype(F32)
        index = lax.broadcasted_iota(jnp.int32, (EXTRA, row_sum.shape[1]), 0)
        low = jnp.where(index == 1, row_sum - high, 0.0)
        out_ref[place:, :] = jnp.where(index == 0, high, low).astype(BF)


def weight_grad(rows, *grads, weights=None):
    count, width = rows.shape
    tile = width // 4
    columns = sum(grad[0].shape[1] for grad in grads) + (EXTRA if weights else 0)
    specs, flat = [], []
    for index, grad in enumerate(grads):
        specs += [resident(part) for part in grad]
        flat += grad
        if weights:
            weight, start = weights[index]
            block = (grad[0].shape[1], tile)
            specs.append(pl.BlockSpec(block, lambda i, start=start: (start, i)))
            flat.append(weight)
    return call(
        functools.partial(weight_grad_kernel, parts=len(grads[0]), summed=bool(weights)),
        "weight_grad",
        4,
        [pl.BlockSpec((count, tile), lambda i: (0, i))] + specs,
        pl.BlockSpec((columns, tile), lambda i: (0, i)),
        jax.ShapeDtypeStruct((columns, width), BF),
        2 * count * width * columns,
    )(rows, *flat)


def norm_back_kernel(sum_ref, x_ref, y_ref, values_ref, base_ref, gain_ref, out_ref, low_ref):
    values = values_ref[...].astype(F32)
    width = values.shape[1]
    grad = sum_ref[...] + x_ref[...].astype(F32) + y_ref[...].astype(F32)
    inverse = lax.rsqrt(jnp.sum(values * values, axis=-1, keepdims=True) / width + EPS)
    gained = grad * gain_ref[...]
    inner = jnp.sum(gained * values, axis=-1, keepdims=True)
    scale = inverse * inverse * inverse * inner / width
    total = base_ref[...].astype(F32) + inverse * gained - values * scale
    out_ref[...] = total
    low_ref[...] = total.astype(BF)


def norm_back(chip, received, values, base, gain):
    rows, width = values.shape
    tile = row_tile(rows // 4, width)
    return call(
        norm_back_kernel,
        "norm_back",
        4,
        [tile] * 5 + [resident(gain)],
        [tile, tile],
        [jax.ShapeDtypeStruct((rows, width), F32), jax.ShapeDtypeStruct((rows, width), BF)],
        1000 * rows * width,
    )(chip, *received, values, base, gain)


def out_grad_kernel(rows_ref, grad_ref, out_ref, *, small):
    product = tn(rows_ref[...], grad_ref[...]).astype(BF)
    tile = product.shape[1]
    for group in range(product.shape[0] // small):
        out_ref[:, group * tile : (group + 1) * tile] = product[group * small : (group + 1) * small]


def out_grad(rows, grad, small, pieces):
    count, columns = rows.shape
    width = grad.shape[1]
    tile = width // pieces
    return call(
        functools.partial(out_grad_kernel, small=small),
        "out_grad",
        pieces,
        [resident(rows), pl.BlockSpec((count, tile), lambda i: (0, i))],
        row_tile(small, columns // small * tile),
        jax.ShapeDtypeStruct((pieces * small, columns // small * tile), BF),
        2 * count * width * columns,
    )(rows, grad)


def per_device(
    residual,
    cotangent,
    attn_gain,
    query_weight,
    key_weight,
    value_weight,
    out_weight,
    ffn_gain,
    gate_weight,
    up_weight,
    down_weight,
):
    dp_size = lax.axis_size("dp")
    seq_size = lax.axis_size("seq")
    count = dp_size * seq_size
    planes = dp_size // 2
    rank = lax.axis_index("seq")
    is_first = lax.axis_index("dp") % 2 == 0
    first_core = rank % 2 == 0
    place = jnp.full((1,), rank, jnp.int32)
    tokens = residual.shape[1]
    width = residual.shape[2]
    small = query_weight.shape[0]
    rows_ffn = gate_weight.shape[0]
    head_cols = query_weight.shape[1] // 8
    hidden_half = gate_weight.shape[1] // 2

    out_moves = [(k, (k % planes) * 8 + k // planes) for k in range(count)]
    plane_out = lax.ppermute(out_weight, AXES, out_moves)

    own_kv = jnp.stack(
        [key_weight.reshape(small, 4, HD), value_weight.reshape(small, 4, HD)], axis=2
    ).reshape(small, 8, HD)
    gains = jnp.pad(jnp.stack([attn_gain, ffn_gain], axis=1), ((0, 0), (0, EXTRA - 2)))
    gains = jnp.broadcast_to(gains[:, None], (small, 8, EXTRA))
    send = jnp.concatenate([query_weight.reshape(small, 8, head_cols), own_kv, gains], axis=2)
    plane_qkv = exchange_plane(send.swapaxes(0, 1)).reshape(8 * small, -1).T
    pieces = width // (8 * small)

    def pack_out(rows):
        return rows.reshape(small, pieces, 8 * small).swapaxes(0, 1).reshape(pieces * small, -1)

    def unpack_out(rows, groups):
        blocks = rows.reshape(pieces, small, groups, 8 * small)
        return blocks.transpose(2, 1, 0, 3).reshape(groups * small, -1)

    packed = gather_z(
        jnp.concatenate([plane_qkv[:head_cols], pack_out(plane_out), plane_qkv[head_cols:]], axis=0)
    )

    def halves(weights):
        parts = [(w[:hidden_half], w[hidden_half:]) for w in weights]
        mine = jnp.concatenate([jnp.where(is_first, left, right) for left, right in parts], axis=0)
        theirs = jnp.concatenate([jnp.where(is_first, right, left) for left, right in parts], axis=0)
        return jnp.concatenate(pick(is_first, mine, flip(theirs, 4)), axis=1)

    row_pieces = gather_plane(after(residual[0], plane_qkv))
    gate_late, up_late = lax.optimization_barrier((gate_weight, up_weight, *row_pieces[6:8]))[:2]
    half_two = halves([gate_late.T, up_late.T])
    w_two = gather_z(half_two)
    cot_rows = cotangent[0]
    half = tokens // 2
    cot_early = after(cot_rows, *row_pieces[8:])
    cot_y = flip(cot_early, 2)
    cot_x = flip(cot_early, 4)
    tables = rotary_tables(tokens * seq_size)
    half_two, tables = lax.optimization_barrier((half_two, tables))
    packed, row_pieces = lax.optimization_barrier((packed, row_pieces, half_two))[:2]

    w_out = unpack_out(packed[head_cols : 2 * head_cols], planes)
    own_half = packed[2 * head_cols : 2 * head_cols + HD]
    gain_row = 2 * head_cols + HD
    gain_one = packed[gain_row : gain_row + 1].astype(F32)
    gain_two = packed[gain_row + 1 : gain_row + 2].astype(F32)
    nothing = jnp.zeros_like(own_half)
    w_kv = jnp.concatenate(
        [jnp.where(first_core, own_half, nothing), jnp.where(first_core, nothing, own_half)], axis=0
    )
    normed_one, queries, kv = project(row_pieces, gain_one, packed, w_kv)
    kv_other = flip(kv, 1)
    queries, cot_y, cot_x = lax.optimization_barrier((queries, cot_y, cot_x))
    cot_top = flip(cot_x[:half], 2)
    cot_low = flip(cot_y[half:], 4)
    half_down = halves([after(down_weight, cot_y).T])
    w_down = gather_z(half_down)
    attended, lse = attend(queries, kv, kv_other, tables, place)
    attended, cot_top, cot_low = lax.optimization_barrier((attended, cot_top, cot_low, half_down))[:3]
    part_rows = attended.shape[0] // 2
    state = scatter_start(
        nn(attended[:part_rows], w_out).astype(BF), nn(attended[part_rows:], w_out).astype(BF)
    )
    sent = scatter_middle(state)
    cot_chip = [after(cot_rows, *sent), cot_y, cot_x, cot_top, cot_low]
    cot_all = jnp.concatenate([flip(piece, 1) for piece in cot_chip] + cot_chip, axis=0)
    branch = scatter_sum(state, scatter_end(state, sent))
    branch, cot_all = lax.optimization_barrier((branch, cot_all))
    stream = residual[0].astype(F32)
    middle = stream + branch
    inverse_two = lax.rsqrt(jnp.mean(middle * middle, axis=-1, keepdims=True) + EPS)

    normed_two, hidden, by_gate, by_up = ffn_hidden(
        gather_plane((middle * inverse_two * gain_two).astype(BF)), w_two
    )
    term_down = weight_grad(cot_all, [hidden])
    sum_down = scatter_z(term_down)
    by_gate = after(by_gate, term_down)
    grad_gate_a, grad_up_a, theirs = ffn_back(cot_all, by_gate, by_up, w_down, w_two, 0)
    grad_gate_b, grad_up_b, mine = ffn_back(cot_all, by_gate, by_up, w_down, w_two, 1)
    state = scatter_start(theirs, mine, True)
    sent = scatter_middle(state)
    term_two = weight_grad(
        after(normed_two, state[2]),
        [grad_gate_a, grad_gate_b],
        [grad_up_a, grad_up_b],
        weights=[(w_two, 0), (w_two, 1)],
    )
    sum_two = scatter_z(term_two)
    received = scatter_end(state, sent)
    received, sum_down = lax.optimization_barrier((received, sum_down, term_two))[:2]
    def own_rows(term):
        first, second = term[:, :rows_ffn], term[:, rows_ffn:]
        other = flip(jnp.where(is_first, second, first), 4)
        return pick(is_first, jnp.where(is_first, first, second), other)

    grad_middle, grad_branch = norm_back(state[0][0], received, middle, cot_rows, gain_two)
    grad_branch = gather_plane(grad_branch)

    hidden_late = after(hidden, grad_middle)
    feed_state = scatter_start(
        nn(hidden_late[:part_rows], w_down).astype(BF), nn(hidden_late[part_rows:], w_down).astype(BF)
    )

    w_out = after(w_out, feed_state[2])
    grad_branch, grad_attended = gathered_dot(grad_branch, w_out)
    term_out = out_grad(attended, grad_branch, small, pieces)
    relayed, grad_attended = lax.optimization_barrier((feed_state[1], grad_attended))
    feed_state = (feed_state[0], relayed, feed_state[2])
    feed_sent = scatter_middle(feed_state)
    grad_attended, feed_sent = lax.optimization_barrier((grad_attended, feed_sent, term_out))[:2]
    feed_received = scatter_end(feed_state, feed_sent)
    grad_q, grad_kv = attend_back(queries, kv, kv_other, grad_attended, lse, tables, place)
    grad_q, grad_kv, feed_received = lax.optimization_barrier((grad_q, grad_kv, feed_received))
    kv_back = flip(grad_kv, 1)
    kv_back = jnp.concatenate([kv_back[part_rows:], kv_back[:part_rows]], axis=0)
    grad_kv = (grad_kv + kv_back).astype(BF)
    term_qkv = weight_grad(normed_one, [grad_q], [grad_kv], weights=[(packed, 0), (w_kv, 0)])
    key_row = head_cols + HD
    value_row = key_row + HD
    term_kv = jnp.where(first_core, term_qkv[head_cols:key_row], term_qkv[key_row:value_row])
    feed = scatter_sum(feed_state, feed_received)
    total_out = middle + feed
    squares = jnp.stack(
        [
            jnp.sum(stream * stream),
            jnp.sum(branch * branch),
            jnp.sum(feed * feed),
            jnp.sum(total_out * total_out),
        ]
    )
    spread = jnp.tile(jnp.pad(squares, (0, small - 4)), width // small)
    high = spread.astype(BF)
    low = (spread - high.astype(F32)).astype(BF)
    squares_rows = jnp.pad(jnp.stack([high, low]), ((2, EXTRA - 4), (0, 0)))
    term_qkv = jnp.concatenate(
        [term_qkv[:head_cols], term_out, term_kv, term_qkv[value_row:] + squares_rows], axis=0
    )
    sums = scatter_z(term_qkv)
    two_first, two_second = own_rows(sum_two[: 2 * hidden_half])
    down_first, down_second = own_rows(sum_down)
    late_q, late_kv = lax.optimization_barrier((grad_q, grad_kv, term_qkv, sum_two))[:2]
    late = jnp.concatenate([late_q, late_kv], axis=1)
    w_qkv = jnp.concatenate([packed[:head_cols], w_kv], axis=0)
    state = scatter_start(
        nn(late[:part_rows], w_qkv).astype(BF), nn(late[part_rows:], w_qkv).astype(BF)
    )
    sent = scatter_middle(state)
    sent, two_first, two_second = lax.optimization_barrier((sent, two_first, two_second))
    received = scatter_end(state, sent)
    grad_stream = norm_back(state[0][0], received, residual[0], grad_middle, gain_one)[0]

    grad_down_w = jnp.concatenate([down_first, down_second], axis=0).T.astype(F32)
    grad_gate_w = jnp.concatenate([two_first[:hidden_half], two_second[:hidden_half]], axis=0).T
    grad_up_w = jnp.concatenate([two_first[hidden_half:], two_second[hidden_half:]], axis=0).T
    grad_gate_w, grad_up_w = grad_gate_w.astype(F32), grad_up_w.astype(F32)
    ready = (grad_stream, total_out, grad_down_w, grad_gate_w, grad_up_w)
    sums, ready = lax.optimization_barrier((sums, ready))
    grad_stream, total_out, grad_down_w, grad_gate_w, grad_up_w = ready

    plane_grad = jnp.concatenate(
        [sums[:head_cols], sums[2 * head_cols :], sum_two[2 * hidden_half :]], axis=0
    ).T
    back = exchange_plane(plane_grad.reshape(8, small, -1))
    grad_out_rows = unpack_out(sums[head_cols : 2 * head_cols], 1)
    grad_out_w = lax.ppermute(grad_out_rows, AXES, [(b, a) for a, b in out_moves]).astype(F32)
    back = back.swapaxes(0, 1).astype(F32)
    row_sums = jnp.sum(back[:, :, head_cols + HD :], axis=1)
    rms_stats = jnp.sqrt(jnp.sum(row_sums[:4, 2:4], axis=1) / (tokens * count * width))
    grad_attn_gain = jnp.sum(row_sums[:, :2], axis=1) / attn_gain.astype(F32)
    grad_ffn_gain = jnp.sum(row_sums[:, EXTRA : EXTRA + 2], axis=1) / ffn_gain.astype(F32)
    back_kv = back[:, :, head_cols : head_cols + HD].reshape(small, 4, 2, HD)
    return (
        total_out.astype(BF)[None],
        grad_stream[None],
        grad_attn_gain,
        back[:, :, :head_cols].reshape(small, -1),
        back_kv[:, :, 0].reshape(small, -1),
        back_kv[:, :, 1].reshape(small, -1),
        grad_out_w,
        grad_ffn_gain,
        grad_gate_w,
        grad_up_w,
        grad_down_w,
        rms_stats,
    )


def solution(mesh):
    token_spec = P("dp", "seq", None)
    gain_spec = P(("dp", "seq"))
    row_spec = P(("dp", "seq"), None)
    ffn_spec = P("dp", "seq")
    weight_specs = (gain_spec, row_spec, row_spec, row_spec, row_spec, gain_spec) + (ffn_spec,) * 3
    return jax.shard_map(
        per_device,
        mesh=mesh,
        in_specs=(token_spec, token_spec) + weight_specs,
        out_specs=(token_spec, token_spec) + weight_specs + (P(),),
        check_vma=False,
    )
```

```python
import functools
import math

import jax
import jax.numpy as jnp
from jax import lax
from jax.experimental import pallas as pl
from jax.experimental.pallas import tpu as pltpu
from jax.sharding import PartitionSpec as P

HD = 64
EPS = 1e-05
AXES = ("dp", "seq")
BF = jnp.bfloat16
F32 = jnp.float32
NEG = -1e30
ROWS = 256
VMEM = 56 << 20
EXTRA = 16
UNPRICED = ("project", "ffn_hidden", )


def after(value, *others):
    return lax.optimization_barrier((value,) + others)[0]


def flip(value, mask):
    count = lax.axis_size("dp") * lax.axis_size("seq")
    return lax.ppermute(value, AXES, [(k, k ^ mask) for k in range(count)])


def column_groups():
    size = lax.axis_size("dp")
    return [list(range(start, size, 2)) for start in range(2)]


def gather_z(value):
    return lax.all_gather(value, "dp", axis=1, tiled=True, axis_index_groups=column_groups())


def scatter_z(value):
    return lax.psum_scatter(
        value, "dp", scatter_dimension=1, tiled=True, axis_index_groups=column_groups()
    )


def pick(is_first, own, other):
    return (jnp.where(is_first, own, other), jnp.where(is_first, other, own))


def gather_plane(block, meanwhile=None, before=()):
    half = block.shape[0] // 2
    from_y = flip(block, 2)
    from_x = flip(block, 4)
    groups = [[block, flip(block, 1)]]
    results = []
    if meanwhile is not None:
        results.append(meanwhile(groups[0], 0))
    if before or results:
        from_y, from_x = lax.optimization_barrier((from_y, from_x, before, results))[:2]
    top = flip(from_x[:half], 2)
    low = flip(from_y[half:], 4)
    groups.append([from_y, flip(from_y, 1), from_x, flip(from_x, 1)])
    if meanwhile is not None:
        results.append(meanwhile(groups[1], 1))
        top, low = lax.optimization_barrier((top, low, results[-1]))[:2]
    groups.append([top, low, flip(top, 1), flip(low, 1)])
    if meanwhile is not None:
        results.append(meanwhile(groups[2], 2))
    return (groups, results)


def chip_sum(part, *others):
    mine, theirs = part
    if others:
        theirs = after(theirs, *others)
    return mine.astype(F32) + flip(theirs, 1).astype(F32)


def scatter_relay(diagonal):
    cross = chip_sum(diagonal).astype(BF)
    half = cross.shape[0] // 2
    return (flip(cross[:half], 2), flip(cross[half:], 4), cross)


def scatter_middle(to_y, to_x, relayed):
    top, low = relayed[:2]
    half = top.shape[0]
    to_x = jnp.concatenate([to_x[:half] + top.astype(F32), to_x[half:]], axis=0).astype(BF)
    to_y = jnp.concatenate([to_y[:half], to_y[half:] + low.astype(F32)], axis=0).astype(BF)
    return (to_x, to_y)


def scatter_end(sent):
    return (flip(sent[0], 4), flip(sent[1], 2))


def exchange_plane(parts):
    rank = (lax.axis_index("dp") % 2) * 4 + lax.axis_index("seq")
    got = [lax.dynamic_index_in_dim(parts, rank, 0, keepdims=False)]
    for mask in range(1, 8):
        got.append(flip(lax.dynamic_index_in_dim(parts, rank ^ mask, 0, keepdims=False), mask))
    for bit in (1, 2, 4):
        odd = (rank & bit) != 0
        got = [jnp.where(odd, got[k ^ bit], got[k]) for k in range(8)]
    return jnp.stack(got)


def plane_place(sequence, block, rank):
    return sequence * 4 + (block ^ rank)


def nt(left, right):
    return lax.dot_general(left, right, (((1,), (1,)), ((), ())), preferred_element_type=F32)


def nn(left, right):
    return lax.dot_general(left, right, (((1,), (0,)), ((), ())), preferred_element_type=F32)


def tn(left, right):
    return lax.dot_general(left, right, (((0,), (0,)), ((), ())), preferred_element_type=F32)


def turn(values, cosine, sine):
    lane = lax.broadcasted_iota(jnp.int32, values.shape, 1)
    partner = jnp.where(lane % HD < HD // 2, pltpu.roll(values, 96, 1), pltpu.roll(values, 32, 1))
    return values * cosine + partner * sine


def twice(values):
    lane = lax.broadcasted_iota(jnp.int32, values.shape, 1)
    swapped = pltpu.roll(values, HD, 1)
    return (jnp.where(lane < HD, values, swapped), jnp.where(lane < HD, swapped, values))


def per_head(values):
    lane = lax.broadcasted_iota(jnp.int32, values.shape, 1)
    zero = jnp.zeros_like(values)
    return jnp.concatenate(
        [jnp.where(lane < HD, values, zero), jnp.where(lane < HD, zero, values)], axis=0
    )


def join_heads(turned):
    back = turned.T
    lane = lax.broadcasted_iota(jnp.int32, (ROWS, 2 * HD), 1)
    return jnp.where(lane < HD, back[:ROWS], back[ROWS:])


def causal(scores):
    place = lax.broadcasted_iota(jnp.int32, scores.shape, 0)
    query = lax.broadcasted_iota(jnp.int32, scores.shape, 1) % ROWS
    return place <= query


def place_rows(ref, place):
    return ref[pl.ds(pl.multiple_of(place * ROWS, ROWS), ROWS), :]


def attend_kernel(rank_ref, q_ref, kv_ref, other_ref, cos_ref, sin_ref, kcos_ref, ksin_ref, out_ref, lse_ref, kk_ref, vt_ref):
    sequence, block = pl.program_id(0), pl.program_id(1)
    blocks = kk_ref.shape[0] // ROWS

    @pl.when(block == 0)
    def _():
        for i in range(blocks):
            place = plane_place(sequence, i, rank_ref[0])
            keys = pl.ds(i * ROWS, ROWS)
            rows = place_rows(kv_ref, place) + place_rows(other_ref, place ^ 1)
            kk, vv = twice(turn(rows, kcos_ref[keys, :], ksin_ref[keys, :]))
            kk_ref[keys, :] = kk.astype(BF)
            vt_ref[:, keys] = vv.T.astype(BF)

    def rows(count):
        for pair in range(q_ref.shape[1] // (2 * HD)):
            columns = pl.ds(pair * 2 * HD, 2 * HD)
            queries = turn(q_ref[:, columns], cos_ref[...], sin_ref[...]).astype(BF) * 0.125
            both = per_head(queries.astype(BF))
            parts = [nt(kk_ref[pl.ds(i * ROWS, ROWS), :], both) for i in range(count)]
            parts[-1] = jnp.where(causal(parts[-1]), parts[-1], NEG)
            highest = functools.reduce(
                jnp.maximum, [jnp.max(p, axis=0, keepdims=True) for p in parts]
            )
            total = jnp.zeros((1, 2 * ROWS), F32)
            mixed = jnp.zeros((2 * HD, 2 * ROWS), F32)
            for i, part in enumerate(parts):
                weights = jnp.exp(part - highest)
                total = total + jnp.sum(weights, axis=0, keepdims=True)
                mixed = mixed + nn(vt_ref[:, pl.ds(i * ROWS, ROWS)], weights.astype(BF))
            lse_ref[0, pair, 0] = highest + jnp.log(total)
            out_ref[:, columns] = join_heads(mixed / total).astype(BF)

    for count in range(1, blocks + 1):
        pl.when(block == count - 1)(functools.partial(rows, count))


def attention_specs(length, pairs):
    tile = pl.BlockSpec((ROWS, 2 * HD), lambda a, i, j, rank: (plane_place(a, j, rank[0]), i))
    table = pl.BlockSpec((ROWS, 2 * HD), lambda a, i, j, rank: (j, 0))
    whole = pl.BlockSpec((length, 2 * HD), lambda a, i, j, rank: (0, 0))
    both = pl.BlockSpec((2 * length, 2 * HD), lambda a, i, j, rank: (0, 0))
    lse = pl.BlockSpec((1, 1, 1, 1, 2 * ROWS), lambda a, i, j, rank: (a, i, j, 0, 0))
    return (tile, table, whole, both, lse)


def attend(queries, kv, other, tables, rank):
    length = queries.shape[0] // 2
    pairs = queries.shape[1] // (2 * HD)
    blocks = length // ROWS
    tile = pl.BlockSpec((ROWS, pairs * 2 * HD), lambda a, j, rank: (plane_place(a, j, rank[0]), 0))
    table = pl.BlockSpec((ROWS, 2 * HD), lambda a, j, rank: (j, 0))
    whole = pl.BlockSpec((length, 2 * HD), lambda a, j, rank: (0, 0))
    both = pl.BlockSpec((2 * length, 2 * HD), lambda a, j, rank: (0, 0))
    lse = pl.BlockSpec((1, pairs, 1, 1, 2 * ROWS), lambda a, j, rank: (a, 0, j, 0, 0))
    return pl.pallas_call(
        attend_kernel,
        name="attend",
        grid_spec=pltpu.PrefetchScalarGridSpec(
            num_scalar_prefetch=1,
            grid=(2, blocks),
            in_specs=[tile, both, both, table, table, whole, whole],
            out_specs=[tile, lse],
            scratch_shapes=[pltpu.VMEM((length, 2 * HD), BF), pltpu.VMEM((2 * HD, length), BF)],
        ),
        out_shape=[
            jax.ShapeDtypeStruct(queries.shape, BF),
            jax.ShapeDtypeStruct((2, pairs, blocks, 1, 2 * ROWS), F32),
        ],
        compiler_params=pltpu.CompilerParams(vmem_limit_bytes=VMEM),
    )(rank, queries, kv, other, *tables)


def attend_back_kernel(rank_ref, q_ref, kv_ref, other_ref, do_ref, lse_ref, cos_ref, sin_ref, kcos_ref, ksin_ref, dq_ref, dkv_ref, kk_ref, kt_ref, vv_ref, dk_ref, dv_ref):
    sequence, pair, block = pl.program_id(0), pl.program_id(1), pl.program_id(2)
    blocks = kk_ref.shape[0] // ROWS

    @pl.when((pair == 0) & (block == 0))
    def _():
        for i in range(blocks):
            place = plane_place(sequence, i, rank_ref[0])
            keys = pl.ds(i * ROWS, ROWS)
            rows = place_rows(kv_ref, place) + place_rows(other_ref, place ^ 1)
            kk, vv = twice(turn(rows, kcos_ref[keys, :], ksin_ref[keys, :]))
            kk_ref[keys, :] = kk.astype(BF)
            kt_ref[:, keys] = kk.T.astype(BF)
            vv_ref[keys, :] = vv.astype(BF)
        dk_ref[...] = jnp.zeros_like(dk_ref)
        dv_ref[...] = jnp.zeros_like(dv_ref)

    both = per_head((turn(q_ref[...], cos_ref[...], sin_ref[...]).astype(BF) * 0.125).astype(BF))
    grads = per_head(do_ref[...])
    lse = lse_ref[...].reshape(1, 2 * ROWS)

    def rows(count):
        kept = []
        inner = jnp.zeros((1, 2 * ROWS), F32)
        for i in range(count):
            keys = pl.ds(i * ROWS, ROWS)
            weights = jnp.exp(nt(kk_ref[keys, :], both) - lse)
            if i == count - 1:
                weights = jnp.where(causal(weights), weights, 0.0)
            grad_probs = nt(vv_ref[keys, :], grads)
            dv_ref[keys, :] += nn(weights.astype(BF), grads)
            inner = inner + jnp.sum(weights * grad_probs, axis=0, keepdims=True)
            kept.append((weights, grad_probs))
        grad_q = jnp.zeros((2 * HD, 2 * ROWS), F32)
        for i, (weights, grad_probs) in enumerate(kept):
            keys = pl.ds(i * ROWS, ROWS)
            grad_scores = (weights * (grad_probs - inner)).astype(BF)
            dk_ref[keys, :] += nn(grad_scores, both)
            grad_q = grad_q + nn(kt_ref[:, keys], grad_scores)
        dq_ref[...] = turn(join_heads(grad_q) * 0.125, cos_ref[...], -sin_ref[...]).astype(BF)

    for count in range(1, blocks + 1):
        pl.when(block == count - 1)(functools.partial(rows, count))

    @pl.when((pair == pl.num_programs(1) - 1) & (block == blocks - 1))
    def _():
        for i in range(blocks):
            keys = pl.ds(i * ROWS, ROWS)
            dk, dv = dk_ref[keys, :], dv_ref[keys, :]
            lane = lax.broadcasted_iota(jnp.int32, dk.shape, 1)
            joined = jnp.where(lane < HD, dk + pltpu.roll(dk, HD, 1), dv + pltpu.roll(dv, HD, 1))
            place = plane_place(sequence, i, rank_ref[0])
            dkv_ref[pl.ds(pl.multiple_of(place * ROWS, ROWS), ROWS), :] = turn(
                joined, kcos_ref[keys, :], -ksin_ref[keys, :]
            )


def attend_back(queries, kv, other, grad_out, lse_rows, tables, rank):
    length = queries.shape[0] // 2
    pairs = queries.shape[1] // (2 * HD)
    blocks = length // ROWS
    tile, table, whole, both, lse = attention_specs(length, pairs)
    wide = pltpu.VMEM((length, 2 * HD), BF)
    return pl.pallas_call(
        attend_back_kernel,
        name="attend_back",
        cost_estimate=pl.CostEstimate(
            flops=280 * pairs * length * length * HD, transcendentals=0, bytes_accessed=1000
        ),
        grid_spec=pltpu.PrefetchScalarGridSpec(
            num_scalar_prefetch=1,
            grid=(2, pairs, blocks),
            in_specs=[tile, both, both, tile, lse, table, table, whole, whole],
            out_specs=[tile, both],
            scratch_shapes=[wide, pltpu.VMEM((2 * HD, length), BF), wide]
            + [pltpu.VMEM((length, 2 * HD), F32)] * 2,
        ),
        out_shape=[
            jax.ShapeDtypeStruct(queries.shape, BF),
            jax.ShapeDtypeStruct(kv.shape, F32),
        ],
        compiler_params=pltpu.CompilerParams(vmem_limit_bytes=VMEM),
    )(rank, queries, kv, other, grad_out, lse_rows, *tables)


def rotary_tables(length):
    half = HD // 2
    freq = jnp.exp(-math.log(10000.0) * 2.0 * jnp.arange(half, dtype=F32) / HD)
    angles = jnp.arange(length).astype(F32)[:, None] * freq[None, :]
    cosine, sine = jnp.cos(angles), jnp.sin(angles)
    one, zero = jnp.ones((length, HD), F32), jnp.zeros((length, HD), F32)
    return (
        jnp.concatenate([cosine] * 4, axis=1),
        jnp.concatenate([-sine, sine] * 2, axis=1),
        jnp.concatenate([cosine, cosine, one], axis=1),
        jnp.concatenate([-sine, sine, zero], axis=1),
    )


def take_piece(pieces, rows_ref):
    rows = rows_ref.shape[0]
    step = place = 0
    for piece in pieces:

        @pl.when(pl.program_id(0) == step)
        def _(piece=piece, place=place):
            rows_ref[place : place + piece.shape[0], :] = piece[...]

        place += piece.shape[0]
        step, place = step + place // rows, place % rows


def put_block(mine_ref, theirs_ref, value):
    own = pl.program_id(0) % 2 == 0

    @pl.when(own)
    def _():
        mine_ref[...] = value

    @pl.when(jnp.logical_not(own))
    def _():
        theirs_ref[...] = value


def pair_tile(rows, columns):
    return pl.BlockSpec((rows, columns), lambda i: (i // 2, 0))


def pair_shapes(rows, width):
    return [jax.ShapeDtypeStruct((rows, width), BF)] * 2


def resident(array, block=None, place=0):
    shape = array.shape if block is None else block
    return pl.BlockSpec(shape, lambda i: (place, 0), pipeline_mode=pl.Buffered(1))


def row_tile(rows, columns, shift=0):
    return pl.BlockSpec((rows, columns), lambda i: (i + shift, 0))


def call(kernel, name, steps, in_specs, out_specs, out_shape, flops, scratch_shapes=(), aliases={}):
    return pl.pallas_call(
        kernel,
        name=name,
        input_output_aliases=aliases,
        cost_estimate=None if name in UNPRICED else pl.CostEstimate(
            flops=int(flops), transcendentals=0, bytes_accessed=int(flops) // 300
        ),
        grid=(steps,),
        in_specs=in_specs,
        out_specs=out_specs,
        out_shape=out_shape,
        scratch_shapes=scratch_shapes,
        compiler_params=pltpu.CompilerParams(vmem_limit_bytes=VMEM),
    )


def project_kernel(*refs):
    gain_ref, wq_ref, wkv_ref, rows_ref, q_ref, kv_ref, raw_ref = refs[-7:]
    take_piece(refs[:-7], raw_ref)
    rows = raw_ref[...].astype(F32)
    inverse = lax.rsqrt(jnp.mean(rows * rows, axis=-1, keepdims=True) + EPS)
    rows = (rows * inverse * gain_ref[...]).astype(BF)
    rows_ref[...] = rows
    q_ref[...] = nt(rows, wq_ref[...])
    kv_ref[...] = nt(rows, wkv_ref[...])


def project(pieces, gain, packed, w_kv):
    tile, width = pieces[0].shape
    columns = 4 * HD
    return call(
        project_kernel,
        "project",
        8,
        [resident(piece) for piece in pieces]
        + [resident(gain), resident(packed, (columns, width)), resident(w_kv)],
        [row_tile(tile, width), row_tile(tile, columns), row_tile(tile, 2 * HD)],
        [
            jax.ShapeDtypeStruct((8 * tile, width), BF),
            jax.ShapeDtypeStruct((8 * tile, columns), F32),
            jax.ShapeDtypeStruct((8 * tile, 2 * HD), F32),
        ],
        16 * tile * width * 8 * HD,
        [pltpu.VMEM((tile, width), BF)],
    )(*pieces, gain, packed, w_kv)


def gathered_dot_kernel(*refs):
    weight_ref, _, rows_ref, out_ref = refs[-4:]
    take_piece(refs[:-4], rows_ref)
    out_ref[...] = nt(rows_ref[...], weight_ref[...]).astype(BF)


def gathered_dot(pieces, weight, start, whole):
    rows, width = weight.shape[0], weight.shape[1]
    tile = whole.shape[0] // 8
    count = sum(piece.shape[0] for piece in pieces)
    return call(
        gathered_dot_kernel,
        "gathered_dot",
        count // tile,
        [resident(piece) for piece in pieces]
        + [resident(weight), pl.BlockSpec(memory_space=pl.ANY)],
        [row_tile(tile, width), row_tile(tile, rows, start)],
        [jax.ShapeDtypeStruct((count, width), BF), jax.ShapeDtypeStruct(whole.shape, BF)],
        2 * count * width * rows,
        aliases={len(pieces) + 1: 1},
    )(*pieces, weight, whole)


def split_product_kernel(rows_ref, weight_ref, mine_ref, theirs_ref):
    put_block(mine_ref, theirs_ref, nn(rows_ref[...], weight_ref[...]).astype(BF))


def split_product(rows, weight, tile, start, blocks):
    inner, width = weight.shape
    half = blocks // 2 * tile
    return call(
        split_product_kernel,
        "split_product",
        blocks,
        [row_tile(tile, inner, start), resident(weight)],
        [pair_tile(tile, width)] * 2,
        pair_shapes(half, width),
        2 * blocks * tile * inner * width,
    )(rows, weight)


def ffn_hidden_kernel(*refs):
    gate_ref, up_ref, rows_ref, hidden_ref, by_gate_ref, by_up_ref = refs[-6:]
    take_piece(refs[:-6], rows_ref)
    rows = rows_ref[...]
    gate = nt(rows, gate_ref[...])
    up = nt(rows, up_ref[...])
    sigmoid = 1.0 / (1.0 + jnp.exp(-gate))
    silu = gate * sigmoid
    hidden_ref[...] = (silu * up).astype(BF)
    by_gate_ref[...] = (up * sigmoid * (1.0 + gate * (1.0 - sigmoid))).astype(BF)
    by_up_ref[...] = silu.astype(BF)


def ffn_hidden(pieces, w_two, tile):
    width = w_two.shape[1]
    count = sum(piece.shape[0] for piece in pieces)
    columns = w_two.shape[0] // 2
    part = (columns, width)
    return call(
        ffn_hidden_kernel,
        "ffn_hidden",
        count // tile,
        [resident(piece) for piece in pieces] + [resident(w_two, part, 0), resident(w_two, part, 1)],
        [row_tile(tile, width)] + [row_tile(tile, columns)] * 3,
        [jax.ShapeDtypeStruct((count, width), BF)]
        + [jax.ShapeDtypeStruct((count, columns), BF)] * 3,
        4 * count * width * columns,
    )(*pieces, w_two, w_two)


def ffn_back_kernel(*refs, starts):
    groups = [refs[3 * i : 3 * i + 3] for i in range(len(starts))]
    down_ref, gate_ref, up_ref, gg_ref, gu_ref = refs[3 * len(starts) : 3 * len(starts) + 5]
    part_refs = refs[3 * len(starts) + 5 :]
    cot, by_gate, by_up = [ref[...] for ref in groups[0]]
    for start, group in zip(starts[1:], groups[1:]):
        later = pl.program_id(0) >= start
        cot, by_gate, by_up = [
            jnp.where(later, ref[...], value) for ref, value in zip(group, (cot, by_gate, by_up))
        ]
    grad_hidden = nt(cot, down_ref[...])
    grad_gate = (grad_hidden * by_gate.astype(F32)).astype(BF)
    grad_up = (grad_hidden * by_up.astype(F32)).astype(BF)
    gg_ref[...] = grad_gate
    gu_ref[...] = grad_up
    part = nn(grad_gate, gate_ref[...]) + nn(grad_up, up_ref[...])
    part = part.astype(BF)
    step = pl.program_id(0)
    for index, start in enumerate(starts):
        end = starts[index + 1] if index + 1 < len(starts) else pl.num_programs(0)

        @pl.when((step >= start) & (step < end))
        def _(index=index):
            put_block(part_refs[2 * index], part_refs[2 * index + 1], part)


def ffn_back(groups, w_down, w_two, tile):
    width = w_two.shape[1]
    columns = w_down.shape[0]
    part = (columns, width)
    specs, starts, steps = [], [], 0
    part_specs, part_shapes = [], []
    for group in groups:
        blocks = group[0].shape[0] // tile
        place = lambda i, start=steps, last=blocks - 1: (jnp.clip(i - start, 0, last), 0)
        specs += [pl.BlockSpec((tile, array.shape[1]), place) for array in group]
        place = lambda i, start=steps, last=blocks // 2 - 1: (jnp.clip((i - start) // 2, 0, last), 0)
        part_specs += [pl.BlockSpec((tile, width), place)] * 2
        part_shapes += pair_shapes(blocks // 2 * tile, width)
        starts.append(steps)
        steps += blocks
    count = steps * tile
    return call(
        functools.partial(ffn_back_kernel, starts=tuple(starts)),
        "ffn_back",
        steps,
        specs + [resident(w_down), resident(w_two, part, 0), resident(w_two, part, 1)],
        [row_tile(tile, columns)] * 2 + part_specs,
        [jax.ShapeDtypeStruct((count, columns), BF)] * 2 + part_shapes,
        6 * count * width * columns,
    )(*[array for group in groups for array in group], w_down, w_two, w_two)


def weight_grad_kernel(*refs, groups, parts, summed):
    rows, grads, out_ref = refs[:groups], refs[groups:-1], refs[-1]
    width = parts + 1 if summed else parts
    place = 0
    row_sum = 0.0
    for start in range(0, len(grads), width):
        total = 0.0
        source, row = 0, 0
        for rows_ref in rows:
            count = rows_ref.shape[0]
            if row == grads[start + source].shape[0]:
                source, row = source + 1, 0
            grad = grads[start + source][row : row + count, :]
            total = total + tn(rows_ref[...], grad)
            row += count
        total = total.T
        columns = total.shape[0]
        if summed:
            weight = grads[start + parts][...].astype(F32)
            row_sum = row_sum + jnp.sum(total * weight, axis=0, keepdims=True)
        out_ref[place : place + columns, :] = total.astype(BF)
        place += columns
    if summed:
        high = row_sum.astype(BF).astype(F32)
        index = lax.broadcasted_iota(jnp.int32, (EXTRA, row_sum.shape[1]), 0)
        low = jnp.where(index == 1, row_sum - high, 0.0)
        out_ref[place:, :] = jnp.where(index == 0, high, low).astype(BF)


def weight_grad(rows, *grads, weights=None):
    width = rows[0].shape[1]
    tile = width // 4
    count = sum(group.shape[0] for group in rows)
    columns = sum(grad[0].shape[1] for grad in grads) + (EXTRA if weights else 0)
    specs = [pl.BlockSpec((group.shape[0], tile), lambda i: (0, i)) for group in rows]
    flat = list(rows)
    for index, grad in enumerate(grads):
        specs += [resident(part) for part in grad]
        flat += grad
        if weights:
            weight, start = weights[index]
            block = (grad[0].shape[1], tile)
            specs.append(pl.BlockSpec(block, lambda i, start=start: (start, i)))
            flat.append(weight)
    return call(
        functools.partial(
            weight_grad_kernel, groups=len(rows), parts=len(grads[0]), summed=bool(weights)
        ),
        "weight_grad",
        4,
        specs,
        pl.BlockSpec((columns, tile), lambda i: (0, i)),
        jax.ShapeDtypeStruct((columns, width), BF),
        2 * count * width * columns,
    )(*flat)


def norm_back_kernel(sum_ref, x_ref, y_ref, values_ref, base_ref, gain_ref, out_ref, low_ref):
    values = values_ref[...].astype(F32)
    width = values.shape[1]
    grad = sum_ref[...] + x_ref[...].astype(F32) + y_ref[...].astype(F32)
    inverse = lax.rsqrt(jnp.sum(values * values, axis=-1, keepdims=True) / width + EPS)
    gained = grad * gain_ref[...]
    inner = jnp.sum(gained * values, axis=-1, keepdims=True)
    scale = inverse * inverse * inverse * inner / width
    total = base_ref[...].astype(F32) + inverse * gained - values * scale
    out_ref[...] = total
    low_ref[...] = total.astype(BF)


def norm_back(own, received, values, base, gain):
    rows, width = values.shape
    tile = row_tile(rows // 4, width)
    return call(
        norm_back_kernel,
        "norm_back",
        4,
        [tile] * 5 + [resident(gain)],
        [tile, tile],
        [jax.ShapeDtypeStruct((rows, width), F32), jax.ShapeDtypeStruct((rows, width), BF)],
        1000 * rows * width,
    )(own, *received, values, base, gain)


def out_grad_kernel(*refs, small):
    rows_ref, grads, out_ref = refs[0], refs[1:-1], refs[-1]
    product, place = 0.0, 0
    for grad_ref in grads:
        count = grad_ref.shape[0]
        product = product + tn(rows_ref[place : place + count, :], grad_ref[...])
        place += count
    product = product.astype(BF)
    tile = product.shape[1]
    for group in range(product.shape[0] // small):
        out_ref[:, group * tile : (group + 1) * tile] = product[group * small : (group + 1) * small]


def out_grad(rows, grads, small, pieces):
    count, columns = rows.shape
    width = grads[0].shape[1]
    tile = width // pieces
    return call(
        functools.partial(out_grad_kernel, small=small),
        "out_grad",
        pieces,
        [resident(rows)] + [pl.BlockSpec((grad.shape[0], tile), lambda i: (0, i)) for grad in grads],
        row_tile(small, columns // small * tile),
        jax.ShapeDtypeStruct((pieces * small, columns // small * tile), BF),
        2 * count * width * columns,
    )(rows, *grads)


def per_device(
    residual,
    cotangent,
    attn_gain,
    query_weight,
    key_weight,
    value_weight,
    out_weight,
    ffn_gain,
    gate_weight,
    up_weight,
    down_weight,
):
    dp_size = lax.axis_size("dp")
    seq_size = lax.axis_size("seq")
    count = dp_size * seq_size
    planes = dp_size // 2
    rank = lax.axis_index("seq")
    is_first = lax.axis_index("dp") % 2 == 0
    first_core = rank % 2 == 0
    place = jnp.full((1,), rank, jnp.int32)
    tokens = residual.shape[1]
    width = residual.shape[2]
    small = query_weight.shape[0]
    rows_ffn = gate_weight.shape[0]
    head_cols = query_weight.shape[1] // 8
    hidden_half = gate_weight.shape[1] // 2

    out_moves = [(k, (k % planes) * 8 + k // planes) for k in range(count)]
    plane_out = lax.ppermute(out_weight, AXES, out_moves)

    own_kv = jnp.stack(
        [key_weight.reshape(small, 4, HD), value_weight.reshape(small, 4, HD)], axis=2
    ).reshape(small, 8, HD)
    gains = jnp.pad(jnp.stack([attn_gain, ffn_gain], axis=1), ((0, 0), (0, EXTRA - 2)))
    gains = jnp.broadcast_to(gains[:, None], (small, 8, EXTRA))
    send = jnp.concatenate([query_weight.reshape(small, 8, head_cols), own_kv, gains], axis=2)
    plane_qkv = exchange_plane(send.swapaxes(0, 1)).reshape(8 * small, -1).T
    pieces = width // (8 * small)

    def pack_out(rows):
        return rows.reshape(small, pieces, 8 * small).swapaxes(0, 1).reshape(pieces * small, -1)

    def unpack_out(rows, groups):
        blocks = rows.reshape(pieces, small, groups, 8 * small)
        return blocks.transpose(2, 1, 0, 3).reshape(groups * small, -1)

    own_packed = jnp.concatenate(
        [plane_qkv[:head_cols], pack_out(plane_out), plane_qkv[head_cols:]], axis=0
    )
    packed = gather_z(own_packed)

    def halves(weights):
        parts = [(w[:hidden_half], w[hidden_half:]) for w in weights]
        mine = jnp.concatenate([jnp.where(is_first, left, right) for left, right in parts], axis=0)
        theirs = jnp.concatenate([jnp.where(is_first, right, left) for left, right in parts], axis=0)
        return jnp.concatenate(pick(is_first, mine, flip(theirs, 4)), axis=1)

    half_two = halves([gate_weight.T, up_weight.T])
    tables = rotary_tables(tokens * seq_size)
    row_groups = gather_plane(after(residual[0], own_packed), before=(half_two, tables))[0]
    w_two = gather_z(after(half_two, packed))
    cot_rows = cotangent[0]
    half = tokens // 2
    cot_early = after(cot_rows, *row_groups[2][:2])
    cot_y = flip(cot_early, 2)
    cot_x = flip(cot_early, 4)
    packed, row_groups = lax.optimization_barrier((packed, row_groups))

    w_out = unpack_out(packed[head_cols : 2 * head_cols], planes)
    own_half = packed[2 * head_cols : 2 * head_cols + HD]
    gain_row = 2 * head_cols + HD
    gain_one = packed[gain_row : gain_row + 1].astype(F32)
    gain_two = packed[gain_row + 1 : gain_row + 2].astype(F32)
    nothing = jnp.zeros_like(own_half)
    w_kv = jnp.concatenate(
        [jnp.where(first_core, own_half, nothing), jnp.where(first_core, nothing, own_half)], axis=0
    )
    row_pieces = row_groups[0] + row_groups[1] + row_groups[2]
    normed_one, queries, kv = project(row_pieces, gain_one, packed, w_kv)
    kv_other = flip(kv, 1)
    attended, lse = attend(queries, kv, kv_other, tables, place)
    half_down = halves([after(down_weight, queries).T])
    w_down = gather_z(half_down)
    attended, cot_y, cot_x = lax.optimization_barrier((attended, cot_y, cot_x, half_down))[:3]

    def scatter_rows(rows, weight):
        block = lambda i: nn(rows[i * tokens : (i + 1) * tokens], weight).astype(BF)
        theirs = block(7)
        relayed = scatter_relay((block(6), theirs))
        rows = after(rows, relayed[2])
        theirs = (block(3), block(5))
        chip_y, chip_x = chip_sum((block(2), theirs[0])), chip_sum((block(4), theirs[1]))
        sent = scatter_middle(chip_y, chip_x, relayed)
        rows = after(rows, *sent)
        theirs = block(1)
        return (sent, chip_sum((block(0), theirs)))

    sent, own = scatter_rows(attended, w_out)
    cot_own = [after(cot_rows, *sent), flip(after(cot_rows, *sent), 1)]
    cot_near = [cot_y, flip(cot_y, 1), cot_x, flip(cot_x, 1)]
    cots = [jnp.concatenate(cot_own, axis=0), jnp.concatenate(cot_near, axis=0)]
    received = scatter_end(sent)
    branch = own + received[0].astype(F32) + received[1].astype(F32)
    branch, cots = lax.optimization_barrier((branch, cots))
    stream = residual[0].astype(F32)
    middle = stream + branch
    inverse_two = lax.rsqrt(jnp.mean(middle * middle, axis=-1, keepdims=True) + EPS)

    squares = [jnp.sum(rows * rows) for rows in (stream, branch)]
    groups, results = gather_plane(
        (middle * inverse_two * gain_two).astype(BF),
        lambda group, _: ffn_hidden(group, w_two, tokens),
        tuple(squares),
    )
    normed_two, hidden, by_gate, by_up = zip(*results)
    cot_top, cot_low = lax.optimization_barrier((cot_x[:half], cot_y[half:], groups[2][:2]))[:2]
    cot_far = lax.optimization_barrier(((flip(cot_top, 2), flip(cot_low, 4)), hidden[2]))[0]
    cot_far = list(cot_far)
    cots.append(jnp.concatenate(cot_far + [flip(piece, 1) for piece in cot_far], axis=0))
    term_down = weight_grad(cots, hidden)
    sum_down = scatter_z(term_down)

    def back(which, *others):
        groups = [(cots[i], by_gate[i], by_up[i]) for i in which]
        groups = lax.optimization_barrier((groups, term_down, others))[0]
        return ffn_back(groups, w_down, w_two, tokens)

    gate_outer, up_outer, *parts = back((1, 2))
    relayed = scatter_relay(parts[2:])
    gate_own, up_own, *own = back((0,), relayed[2])
    chip = chip_sum(parts[:2])
    sent = scatter_middle(chip[:tokens], chip[tokens:], relayed)
    kept = lax.optimization_barrier((normed_two, sent))[0]
    kept = list(kept)
    term_two = weight_grad(
        kept, [gate_own, gate_outer], [up_own, up_outer], weights=[(w_two, 0), (w_two, 1)]
    )
    sum_two = scatter_z(term_two)
    received = lax.optimization_barrier((scatter_end(sent), term_two))[0]
    own = chip_sum(own, *received)

    def own_rows(term):
        first, second = term[:, :rows_ffn], term[:, rows_ffn:]
        other = flip(jnp.where(is_first, second, first), 4)
        return pick(is_first, jnp.where(is_first, first, second), other)

    grad_middle, grad_branch = norm_back(own, received, middle, cot_rows, gain_two)
    whole = jnp.zeros(attended.shape, BF)
    feed_near = split_product(after(hidden[1], grad_middle), w_down, tokens, 0, 4)
    feed_far = split_product(after(hidden[2], grad_middle), w_down, tokens, 0, 2)
    groups = gather_plane(grad_branch, before=(feed_near, feed_far))[0]
    feed_own = split_product(after(hidden[0], feed_near, feed_far, sum_down), w_down, tokens, 0, 2)

    w_out = lax.optimization_barrier((w_out, feed_own))[0]
    near, whole = gathered_dot(groups[0] + groups[1], w_out, 0, whole)
    far, whole = gathered_dot(groups[2], w_out, 6, whole)
    grad_branch = [near, far]
    relayed = scatter_relay(feed_far)
    term_out = out_grad(attended, grad_branch, small, pieces)
    relayed = lax.optimization_barrier((relayed, term_out))[0]
    chip = chip_sum(feed_near)
    feed_sent = scatter_middle(chip[:tokens], chip[tokens:], relayed)
    down_first, down_second = own_rows(sum_down)
    grad_down_w = jnp.concatenate([down_first, down_second], axis=0).T.astype(F32)
    whole, feed_sent = lax.optimization_barrier((whole, feed_sent, term_out, down_second))[:2]
    feed_received = scatter_end(feed_sent)
    grad_q, grad_kv = attend_back(queries, kv, kv_other, whole, lse, tables, place)
    grad_q, grad_kv, feed_received = lax.optimization_barrier((grad_q, grad_kv, feed_received))
    kv_back = flip(grad_kv, 1)
    kv_back = kv_back.reshape(4, 2, tokens, -1)[:, ::-1].reshape(kv_back.shape)
    grad_kv = (grad_kv + kv_back).astype(BF)
    term_qkv = weight_grad([normed_one], [grad_q], [grad_kv], weights=[(packed, 0), (w_kv, 0)])
    key_row = head_cols + HD
    value_row = key_row + HD
    term_kv = jnp.where(first_core, term_qkv[head_cols:key_row], term_qkv[key_row:value_row])
    feed = chip_sum(feed_own) + feed_received[0].astype(F32) + feed_received[1].astype(F32)
    total_out = middle + feed
    squares = squares + [jnp.sum(rows * rows) for rows in (feed, total_out)]
    column = lax.broadcasted_iota(jnp.int32, (EXTRA, width), 1) % small
    row = lax.broadcasted_iota(jnp.int32, (EXTRA, width), 0)
    spread = sum(jnp.where(column == k, squares[k], 0.0) for k in range(4))
    high = spread.astype(BF).astype(F32)
    low = jnp.where(row == 3, spread - high, 0.0)
    squares_rows = jnp.where(row == 2, high, low).astype(BF)
    term_qkv = jnp.concatenate(
        [term_qkv[:head_cols], term_out, term_kv, term_qkv[value_row:] + squares_rows], axis=0
    )
    sums = scatter_z(after(term_qkv, sum_two))
    late_q, late_kv = lax.optimization_barrier((grad_q, grad_kv, term_qkv))[:2]
    late = jnp.concatenate([late_q, late_kv], axis=1)
    w_qkv = jnp.concatenate([packed[:head_cols], w_kv], axis=0)
    sent, own = scatter_rows(late, w_qkv)
    received = scatter_end(sent)
    two_first, two_second = own_rows(after(sum_two[: 2 * hidden_half], *received))
    grad_stream = norm_back(own, received, residual[0], grad_middle, gain_one)[0]

    grad_gate_w = jnp.concatenate([two_first[:hidden_half], two_second[:hidden_half]], axis=0).T
    grad_up_w = jnp.concatenate([two_first[hidden_half:], two_second[hidden_half:]], axis=0).T
    grad_gate_w, grad_up_w = grad_gate_w.astype(F32), grad_up_w.astype(F32)
    sums, total_out, grad_down_w = lax.optimization_barrier((sums, total_out, grad_down_w))

    plane_grad = jnp.concatenate(
        [sums[:head_cols], sums[2 * head_cols :], sum_two[2 * hidden_half :]], axis=0
    ).T
    back = exchange_plane(plane_grad.reshape(8, small, -1))
    grad_out_rows = unpack_out(sums[head_cols : 2 * head_cols], 1)
    grad_out_w = lax.ppermute(grad_out_rows, AXES, [(b, a) for a, b in out_moves]).astype(F32)
    back = back.swapaxes(0, 1).astype(F32)
    row_sums = jnp.sum(back[:, :, head_cols + HD :], axis=1)
    rms_stats = jnp.sqrt(jnp.sum(row_sums[:4, 2:4], axis=1) / (tokens * count * width))
    grad_attn_gain = jnp.sum(row_sums[:, :2], axis=1) / attn_gain.astype(F32)
    grad_ffn_gain = jnp.sum(row_sums[:, EXTRA : EXTRA + 2], axis=1) / ffn_gain.astype(F32)
    back_kv = back[:, :, head_cols : head_cols + HD].reshape(small, 4, 2, HD)
    return (
        total_out.astype(BF)[None],
        grad_stream[None],
        grad_attn_gain,
        back[:, :, :head_cols].reshape(small, -1),
        back_kv[:, :, 0].reshape(small, -1),
        back_kv[:, :, 1].reshape(small, -1),
        grad_out_w,
        grad_ffn_gain,
        grad_gate_w,
        grad_up_w,
        grad_down_w,
        rms_stats,
    )


def solution(mesh):
    token_spec = P("dp", "seq", None)
    gain_spec = P(("dp", "seq"))
    row_spec = P(("dp", "seq"), None)
    ffn_spec = P("dp", "seq")
    weight_specs = (gain_spec, row_spec, row_spec, row_spec, row_spec, gain_spec) + (ffn_spec,) * 3
    return jax.shard_map(
        per_device,
        mesh=mesh,
        in_specs=(token_spec, token_spec) + weight_specs,
        out_specs=(token_spec, token_spec) + weight_specs + (P(),),
        check_vma=False,
    )
```

```python
import functools
import math

import jax
import jax.numpy as jnp
from jax import lax
from jax.experimental import pallas as pl
from jax.experimental.pallas import tpu as pltpu
from jax.sharding import PartitionSpec as P

HD = 64
EPS = 1e-05
AXES = ("dp", "seq")
BF = jnp.bfloat16
F32 = jnp.float32
NEG = -1e30
ROWS = 256
VMEM = 56 << 20
EXTRA = 16
UNPRICED = ("project", "ffn_hidden", )


def after(value, *others):
    return lax.optimization_barrier((value,) + others)[0]


def flip(value, mask):
    count = lax.axis_size("dp") * lax.axis_size("seq")
    return lax.ppermute(value, AXES, [(k, k ^ mask) for k in range(count)])


def column_groups():
    size = lax.axis_size("dp")
    return [list(range(start, size, 2)) for start in range(2)]


def gather_z(value):
    return lax.all_gather(value, "dp", axis=1, tiled=True, axis_index_groups=column_groups())


def scatter_z(value):
    return lax.psum_scatter(
        value, "dp", scatter_dimension=1, tiled=True, axis_index_groups=column_groups()
    )


def pick(is_first, own, other):
    return (jnp.where(is_first, own, other), jnp.where(is_first, other, own))


def gather_plane(block, meanwhile=None, before=()):
    half = block.shape[0] // 2
    from_y = flip(block, 2)
    from_x = flip(block, 4)
    groups = [[block, flip(block, 1)]]
    results = []
    if meanwhile is not None:
        results.append(meanwhile(groups[0], 0))
    if before or results:
        from_y, from_x = lax.optimization_barrier((from_y, from_x, before, results))[:2]
    top = flip(from_x[:half], 2)
    low = flip(from_y[half:], 4)
    groups.append([from_y, flip(from_y, 1), from_x, flip(from_x, 1)])
    if meanwhile is not None:
        results.append(meanwhile(groups[1], 1))
        top, low = lax.optimization_barrier((top, low, results[-1]))[:2]
    groups.append([top, low, flip(top, 1), flip(low, 1)])
    if meanwhile is not None:
        results.append(meanwhile(groups[2], 2))
    return (groups, results)


def chip_sum(part, *others):
    mine, theirs = part
    if others:
        theirs = after(theirs, *others)
    return mine.astype(F32) + flip(theirs, 1).astype(F32)


def scatter_relay(diagonal):
    cross = chip_sum(diagonal).astype(BF)
    half = cross.shape[0] // 2
    return (flip(cross[:half], 2), flip(cross[half:], 4), cross)


def scatter_middle(to_y, to_x, relayed):
    top, low = relayed[:2]
    half = top.shape[0]
    to_x = jnp.concatenate([to_x[:half] + top.astype(F32), to_x[half:]], axis=0).astype(BF)
    to_y = jnp.concatenate([to_y[:half], to_y[half:] + low.astype(F32)], axis=0).astype(BF)
    return (to_x, to_y)


def scatter_end(sent):
    return (flip(sent[0], 4), flip(sent[1], 2))


def exchange_plane(parts):
    rank = (lax.axis_index("dp") % 2) * 4 + lax.axis_index("seq")
    got = [lax.dynamic_index_in_dim(parts, rank, 0, keepdims=False)]
    for mask in range(1, 8):
        got.append(flip(lax.dynamic_index_in_dim(parts, rank ^ mask, 0, keepdims=False), mask))
    for bit in (1, 2, 4):
        odd = (rank & bit) != 0
        got = [jnp.where(odd, got[k ^ bit], got[k]) for k in range(8)]
    return jnp.stack(got)


def plane_place(sequence, block, rank):
    return sequence * 4 + (block ^ rank)


def nt(left, right):
    return lax.dot_general(left, right, (((1,), (1,)), ((), ())), preferred_element_type=F32)


def nn(left, right):
    return lax.dot_general(left, right, (((1,), (0,)), ((), ())), preferred_element_type=F32)


def tn(left, right):
    return lax.dot_general(left, right, (((0,), (0,)), ((), ())), preferred_element_type=F32)


def turn(values, cosine, sine):
    lane = lax.broadcasted_iota(jnp.int32, values.shape, 1)
    partner = jnp.where(lane % HD < HD // 2, pltpu.roll(values, 96, 1), pltpu.roll(values, 32, 1))
    return values * cosine + partner * sine


def twice(values):
    lane = lax.broadcasted_iota(jnp.int32, values.shape, 1)
    swapped = pltpu.roll(values, HD, 1)
    return (jnp.where(lane < HD, values, swapped), jnp.where(lane < HD, swapped, values))


def per_head(values):
    lane = lax.broadcasted_iota(jnp.int32, values.shape, 1)
    zero = jnp.zeros_like(values)
    return jnp.concatenate(
        [jnp.where(lane < HD, values, zero), jnp.where(lane < HD, zero, values)], axis=0
    )


def join_heads(turned):
    back = turned.T
    lane = lax.broadcasted_iota(jnp.int32, (ROWS, 2 * HD), 1)
    return jnp.where(lane < HD, back[:ROWS], back[ROWS:])


def causal(scores):
    place = lax.broadcasted_iota(jnp.int32, scores.shape, 0)
    query = lax.broadcasted_iota(jnp.int32, scores.shape, 1) % ROWS
    return place <= query


def place_rows(ref, place):
    return ref[pl.ds(pl.multiple_of(place * ROWS, ROWS), ROWS), :]


def attend_kernel(rank_ref, q_ref, kv_ref, other_ref, cos_ref, sin_ref, kcos_ref, ksin_ref, out_ref, lse_ref, kk_ref, vt_ref):
    sequence, block = pl.program_id(0), pl.program_id(1)
    blocks = kk_ref.shape[0] // ROWS

    @pl.when(block == 0)
    def _():
        for i in range(blocks):
            place = plane_place(sequence, i, rank_ref[0])
            keys = pl.ds(i * ROWS, ROWS)
            rows = place_rows(kv_ref, place) + place_rows(other_ref, place ^ 1)
            kk, vv = twice(turn(rows, kcos_ref[keys, :], ksin_ref[keys, :]))
            kk_ref[keys, :] = kk.astype(BF)
            vt_ref[:, keys] = vv.T.astype(BF)

    def rows(count):
        for pair in range(q_ref.shape[1] // (2 * HD)):
            columns = pl.ds(pair * 2 * HD, 2 * HD)
            queries = turn(q_ref[:, columns], cos_ref[...], sin_ref[...]).astype(BF) * 0.125
            both = per_head(queries.astype(BF))
            parts = [nt(kk_ref[pl.ds(i * ROWS, ROWS), :], both) for i in range(count)]
            parts[-1] = jnp.where(causal(parts[-1]), parts[-1], NEG)
            highest = functools.reduce(
                jnp.maximum, [jnp.max(p, axis=0, keepdims=True) for p in parts]
            )
            total = jnp.zeros((1, 2 * ROWS), F32)
            mixed = jnp.zeros((2 * HD, 2 * ROWS), F32)
            for i, part in enumerate(parts):
                weights = jnp.exp(part - highest)
                total = total + jnp.sum(weights, axis=0, keepdims=True)
                mixed = mixed + nn(vt_ref[:, pl.ds(i * ROWS, ROWS)], weights.astype(BF))
            lse_ref[0, pair, 0] = highest + jnp.log(total)
            out_ref[:, columns] = join_heads(mixed / total).astype(BF)

    for count in range(1, blocks + 1):
        pl.when(block == count - 1)(functools.partial(rows, count))


def attention_specs(length, pairs):
    tile = pl.BlockSpec((ROWS, 2 * HD), lambda a, i, j, rank: (plane_place(a, j, rank[0]), i))
    table = pl.BlockSpec((ROWS, 2 * HD), lambda a, i, j, rank: (j, 0))
    whole = pl.BlockSpec((length, 2 * HD), lambda a, i, j, rank: (0, 0))
    both = pl.BlockSpec((2 * length, 2 * HD), lambda a, i, j, rank: (0, 0))
    lse = pl.BlockSpec((1, 1, 1, 1, 2 * ROWS), lambda a, i, j, rank: (a, i, j, 0, 0))
    return (tile, table, whole, both, lse)


def attend(queries, kv, other, tables, rank):
    length = queries.shape[0] // 2
    pairs = queries.shape[1] // (2 * HD)
    blocks = length // ROWS
    tile = pl.BlockSpec((ROWS, pairs * 2 * HD), lambda a, j, rank: (plane_place(a, j, rank[0]), 0))
    table = pl.BlockSpec((ROWS, 2 * HD), lambda a, j, rank: (j, 0))
    whole = pl.BlockSpec((length, 2 * HD), lambda a, j, rank: (0, 0))
    both = pl.BlockSpec((2 * length, 2 * HD), lambda a, j, rank: (0, 0))
    lse = pl.BlockSpec((1, pairs, 1, 1, 2 * ROWS), lambda a, j, rank: (a, 0, j, 0, 0))
    return pl.pallas_call(
        attend_kernel,
        name="attend",
        grid_spec=pltpu.PrefetchScalarGridSpec(
            num_scalar_prefetch=1,
            grid=(2, blocks),
            in_specs=[tile, both, both, table, table, whole, whole],
            out_specs=[tile, lse],
            scratch_shapes=[pltpu.VMEM((length, 2 * HD), BF), pltpu.VMEM((2 * HD, length), BF)],
        ),
        out_shape=[
            jax.ShapeDtypeStruct(queries.shape, BF),
            jax.ShapeDtypeStruct((2, pairs, blocks, 1, 2 * ROWS), F32),
        ],
        compiler_params=pltpu.CompilerParams(vmem_limit_bytes=VMEM),
    )(rank, queries, kv, other, *tables)


def attend_back_kernel(rank_ref, q_ref, kv_ref, other_ref, do_ref, lse_ref, cos_ref, sin_ref, kcos_ref, ksin_ref, dq_ref, dkv_ref, kk_ref, kt_ref, vv_ref, dk_ref, dv_ref):
    sequence, pair, block = pl.program_id(0), pl.program_id(1), pl.program_id(2)
    blocks = kk_ref.shape[0] // ROWS

    @pl.when((pair == 0) & (block == 0))
    def _():
        for i in range(blocks):
            place = plane_place(sequence, i, rank_ref[0])
            keys = pl.ds(i * ROWS, ROWS)
            rows = place_rows(kv_ref, place) + place_rows(other_ref, place ^ 1)
            kk, vv = twice(turn(rows, kcos_ref[keys, :], ksin_ref[keys, :]))
            kk_ref[keys, :] = kk.astype(BF)
            kt_ref[:, keys] = kk.T.astype(BF)
            vv_ref[keys, :] = vv.astype(BF)
        dk_ref[...] = jnp.zeros_like(dk_ref)
        dv_ref[...] = jnp.zeros_like(dv_ref)

    both = per_head((turn(q_ref[...], cos_ref[...], sin_ref[...]).astype(BF) * 0.125).astype(BF))
    grads = per_head(do_ref[...])
    lse = lse_ref[...].reshape(1, 2 * ROWS)

    def rows(count):
        kept = []
        inner = jnp.zeros((1, 2 * ROWS), F32)
        for i in range(count):
            keys = pl.ds(i * ROWS, ROWS)
            weights = jnp.exp(nt(kk_ref[keys, :], both) - lse)
            if i == count - 1:
                weights = jnp.where(causal(weights), weights, 0.0)
            grad_probs = nt(vv_ref[keys, :], grads)
            dv_ref[keys, :] += nn(weights.astype(BF), grads)
            inner = inner + jnp.sum(weights * grad_probs, axis=0, keepdims=True)
            kept.append((weights, grad_probs))
        grad_q = jnp.zeros((2 * HD, 2 * ROWS), F32)
        for i, (weights, grad_probs) in enumerate(kept):
            keys = pl.ds(i * ROWS, ROWS)
            grad_scores = (weights * (grad_probs - inner)).astype(BF)
            dk_ref[keys, :] += nn(grad_scores, both)
            grad_q = grad_q + nn(kt_ref[:, keys], grad_scores)
        dq_ref[...] = turn(join_heads(grad_q) * 0.125, cos_ref[...], -sin_ref[...]).astype(BF)

    for count in range(1, blocks + 1):
        pl.when(block == count - 1)(functools.partial(rows, count))

    @pl.when((pair == pl.num_programs(1) - 1) & (block == blocks - 1))
    def _():
        for i in range(blocks):
            keys = pl.ds(i * ROWS, ROWS)
            dk, dv = dk_ref[keys, :], dv_ref[keys, :]
            lane = lax.broadcasted_iota(jnp.int32, dk.shape, 1)
            joined = jnp.where(lane < HD, dk + pltpu.roll(dk, HD, 1), dv + pltpu.roll(dv, HD, 1))
            place = plane_place(sequence, i, rank_ref[0])
            dkv_ref[pl.ds(pl.multiple_of(place * ROWS, ROWS), ROWS), :] = turn(
                joined, kcos_ref[keys, :], -ksin_ref[keys, :]
            )


def attend_back(queries, kv, other, grad_out, lse_rows, tables, rank):
    length = queries.shape[0] // 2
    pairs = queries.shape[1] // (2 * HD)
    blocks = length // ROWS
    tile, table, whole, both, lse = attention_specs(length, pairs)
    wide = pltpu.VMEM((length, 2 * HD), BF)
    return pl.pallas_call(
        attend_back_kernel,
        name="attend_back",
        cost_estimate=pl.CostEstimate(
            flops=280 * pairs * length * length * HD, transcendentals=0, bytes_accessed=1000
        ),
        grid_spec=pltpu.PrefetchScalarGridSpec(
            num_scalar_prefetch=1,
            grid=(2, pairs, blocks),
            in_specs=[tile, both, both, tile, lse, table, table, whole, whole],
            out_specs=[tile, both],
            scratch_shapes=[wide, pltpu.VMEM((2 * HD, length), BF), wide]
            + [pltpu.VMEM((length, 2 * HD), F32)] * 2,
        ),
        out_shape=[
            jax.ShapeDtypeStruct(queries.shape, BF),
            jax.ShapeDtypeStruct(kv.shape, F32),
        ],
        compiler_params=pltpu.CompilerParams(vmem_limit_bytes=VMEM),
    )(rank, queries, kv, other, grad_out, lse_rows, *tables)


def rotary_tables(length):
    half = HD // 2
    freq = jnp.exp(-math.log(10000.0) * 2.0 * jnp.arange(half, dtype=F32) / HD)
    angles = jnp.arange(length).astype(F32)[:, None] * freq[None, :]
    cosine, sine = jnp.cos(angles), jnp.sin(angles)
    one, zero = jnp.ones((length, HD), F32), jnp.zeros((length, HD), F32)
    return (
        jnp.concatenate([cosine] * 4, axis=1),
        jnp.concatenate([-sine, sine] * 2, axis=1),
        jnp.concatenate([cosine, cosine, one], axis=1),
        jnp.concatenate([-sine, sine, zero], axis=1),
    )


def take_piece(pieces, rows_ref):
    rows = rows_ref.shape[0]
    step = place = 0
    for piece in pieces:

        @pl.when(pl.program_id(0) == step)
        def _(piece=piece, place=place):
            rows_ref[place : place + piece.shape[0], :] = piece[...]

        place += piece.shape[0]
        step, place = step + place // rows, place % rows


def put_block(mine_ref, theirs_ref, value):
    own = pl.program_id(0) % 2 == 0

    @pl.when(own)
    def _():
        mine_ref[...] = value

    @pl.when(jnp.logical_not(own))
    def _():
        theirs_ref[...] = value


def pair_tile(rows, columns):
    return pl.BlockSpec((rows, columns), lambda i: (i // 2, 0))


def pair_shapes(rows, width):
    return [jax.ShapeDtypeStruct((rows, width), BF)] * 2


def resident(array, block=None, place=0):
    shape = array.shape if block is None else block
    return pl.BlockSpec(shape, lambda i: (place, 0), pipeline_mode=pl.Buffered(1))


def row_tile(rows, columns, shift=0):
    return pl.BlockSpec((rows, columns), lambda i: (i + shift, 0))


def call(kernel, name, steps, in_specs, out_specs, out_shape, flops, scratch_shapes=(), aliases={}):
    return pl.pallas_call(
        kernel,
        name=name,
        input_output_aliases=aliases,
        cost_estimate=None if name in UNPRICED else pl.CostEstimate(
            flops=int(flops), transcendentals=0, bytes_accessed=int(flops) // 300
        ),
        grid=(steps,),
        in_specs=in_specs,
        out_specs=out_specs,
        out_shape=out_shape,
        scratch_shapes=scratch_shapes,
        compiler_params=pltpu.CompilerParams(vmem_limit_bytes=VMEM),
    )


def project_kernel(*refs):
    gain_ref, wq_ref, wkv_ref, rows_ref, q_ref, kv_ref, raw_ref = refs[-7:]
    take_piece(refs[:-7], raw_ref)
    rows = raw_ref[...].astype(F32)
    inverse = lax.rsqrt(jnp.mean(rows * rows, axis=-1, keepdims=True) + EPS)
    rows = (rows * inverse * gain_ref[...]).astype(BF)
    rows_ref[...] = rows
    q_ref[...] = nt(rows, wq_ref[...])
    kv_ref[...] = nt(rows, wkv_ref[...])


def project(pieces, gain, packed, w_kv):
    tile, width = pieces[0].shape
    columns = 4 * HD
    return call(
        project_kernel,
        "project",
        8,
        [resident(piece) for piece in pieces]
        + [resident(gain), resident(packed, (columns, width)), resident(w_kv)],
        [row_tile(tile, width), row_tile(tile, columns), row_tile(tile, 2 * HD)],
        [
            jax.ShapeDtypeStruct((8 * tile, width), BF),
            jax.ShapeDtypeStruct((8 * tile, columns), F32),
            jax.ShapeDtypeStruct((8 * tile, 2 * HD), F32),
        ],
        16 * tile * width * 8 * HD,
        [pltpu.VMEM((tile, width), BF)],
    )(*pieces, gain, packed, w_kv)


def gathered_dot_kernel(*refs):
    weight_ref, _, rows_ref, out_ref = refs[-4:]
    take_piece(refs[:-4], rows_ref)
    out_ref[...] = nt(rows_ref[...], weight_ref[...]).astype(BF)


def gathered_dot(pieces, weight, start, whole):
    rows, width = weight.shape[0], weight.shape[1]
    tile = whole.shape[0] // 8
    count = sum(piece.shape[0] for piece in pieces)
    return call(
        gathered_dot_kernel,
        "gathered_dot",
        count // tile,
        [resident(piece) for piece in pieces]
        + [resident(weight), pl.BlockSpec(memory_space=pl.ANY)],
        [row_tile(tile, width), row_tile(tile, rows, start)],
        [jax.ShapeDtypeStruct((count, width), BF), jax.ShapeDtypeStruct(whole.shape, BF)],
        2 * count * width * rows,
        aliases={len(pieces) + 1: 1},
    )(*pieces, weight, whole)


def split_product_kernel(rows_ref, weight_ref, mine_ref, theirs_ref):
    put_block(mine_ref, theirs_ref, nn(rows_ref[...], weight_ref[...]).astype(BF))


def split_product(rows, weight, tile, start, blocks):
    inner, width = weight.shape
    half = blocks // 2 * tile
    return call(
        split_product_kernel,
        "split_product",
        blocks,
        [row_tile(tile, inner, start), resident(weight)],
        [pair_tile(tile, width)] * 2,
        pair_shapes(half, width),
        2 * blocks * tile * inner * width,
    )(rows, weight)


def ffn_hidden_kernel(*refs):
    gate_ref, up_ref, rows_ref, hidden_ref, by_gate_ref, by_up_ref = refs[-6:]
    take_piece(refs[:-6], rows_ref)
    rows = rows_ref[...]
    gate = nt(rows, gate_ref[...])
    up = nt(rows, up_ref[...])
    sigmoid = 1.0 / (1.0 + jnp.exp(-gate))
    silu = gate * sigmoid
    hidden_ref[...] = (silu * up).astype(BF)
    by_gate_ref[...] = (up * sigmoid * (1.0 + gate * (1.0 - sigmoid))).astype(BF)
    by_up_ref[...] = silu.astype(BF)


def ffn_hidden(pieces, w_two, tile):
    width = w_two.shape[1]
    count = sum(piece.shape[0] for piece in pieces)
    columns = w_two.shape[0] // 2
    part = (columns, width)
    return call(
        ffn_hidden_kernel,
        "ffn_hidden",
        count // tile,
        [resident(piece) for piece in pieces] + [resident(w_two, part, 0), resident(w_two, part, 1)],
        [row_tile(tile, width)] + [row_tile(tile, columns)] * 3,
        [jax.ShapeDtypeStruct((count, width), BF)]
        + [jax.ShapeDtypeStruct((count, columns), BF)] * 3,
        4 * count * width * columns,
    )(*pieces, w_two, w_two)


def ffn_back_kernel(*refs, starts):
    groups = [refs[3 * i : 3 * i + 3] for i in range(len(starts))]
    down_ref, gate_ref, up_ref, gg_ref, gu_ref = refs[3 * len(starts) : 3 * len(starts) + 5]
    part_refs = refs[3 * len(starts) + 5 :]
    cot, by_gate, by_up = [ref[...] for ref in groups[0]]
    for start, group in zip(starts[1:], groups[1:]):
        later = pl.program_id(0) >= start
        cot, by_gate, by_up = [
            jnp.where(later, ref[...], value) for ref, value in zip(group, (cot, by_gate, by_up))
        ]
    grad_hidden = nt(cot, down_ref[...])
    grad_gate = (grad_hidden * by_gate.astype(F32)).astype(BF)
    grad_up = (grad_hidden * by_up.astype(F32)).astype(BF)
    gg_ref[...] = grad_gate
    gu_ref[...] = grad_up
    part = nn(grad_gate, gate_ref[...]) + nn(grad_up, up_ref[...])
    part = part.astype(BF)
    step = pl.program_id(0)
    for index, start in enumerate(starts):
        end = starts[index + 1] if index + 1 < len(starts) else pl.num_programs(0)

        @pl.when((step >= start) & (step < end))
        def _(index=index):
            put_block(part_refs[2 * index], part_refs[2 * index + 1], part)


def ffn_back(groups, w_down, w_two, tile):
    width = w_two.shape[1]
    columns = w_down.shape[0]
    part = (columns, width)
    specs, starts, steps = [], [], 0
    part_specs, part_shapes = [], []
    for group in groups:
        blocks = group[0].shape[0] // tile
        place = lambda i, start=steps, last=blocks - 1: (jnp.clip(i - start, 0, last), 0)
        specs += [pl.BlockSpec((tile, array.shape[1]), place) for array in group]
        place = lambda i, start=steps, last=blocks // 2 - 1: (jnp.clip((i - start) // 2, 0, last), 0)
        part_specs += [pl.BlockSpec((tile, width), place)] * 2
        part_shapes += pair_shapes(blocks // 2 * tile, width)
        starts.append(steps)
        steps += blocks
    count = steps * tile
    return call(
        functools.partial(ffn_back_kernel, starts=tuple(starts)),
        "ffn_back",
        steps,
        specs + [resident(w_down), resident(w_two, part, 0), resident(w_two, part, 1)],
        [row_tile(tile, columns)] * 2 + part_specs,
        [jax.ShapeDtypeStruct((count, columns), BF)] * 2 + part_shapes,
        6 * count * width * columns,
    )(*[array for group in groups for array in group], w_down, w_two, w_two)


def weight_grad_kernel(*refs, groups, parts, summed):
    outs = 2 if summed else 1
    rows, grads, out_ref = refs[:groups], refs[groups:-outs], refs[-outs]
    width = parts + 1 if summed else parts
    place = 0
    row_sum = 0.0
    for start in range(0, len(grads), width):
        total = 0.0
        source, row = 0, 0
        for rows_ref in rows:
            count = rows_ref.shape[0]
            if row == grads[start + source].shape[0]:
                source, row = source + 1, 0
            grad = grads[start + source][row : row + count, :]
            total = total + tn(rows_ref[...], grad)
            row += count
        total = total.T
        columns = total.shape[0]
        if summed:
            weight = grads[start + parts][...].astype(F32)
            row_sum = row_sum + jnp.sum(total * weight, axis=0, keepdims=True)
        out_ref[place : place + columns, :] = total.astype(BF)
        place += columns
    if summed:
        refs[-1][...] = jnp.broadcast_to(row_sum, refs[-1].shape)


def weight_grad(rows, *grads, weights=None):
    width = rows[0].shape[1]
    tile = width // 4
    count = sum(group.shape[0] for group in rows)
    columns = sum(grad[0].shape[1] for grad in grads)
    specs = [pl.BlockSpec((group.shape[0], tile), lambda i: (0, i)) for group in rows]
    flat = list(rows)
    for index, grad in enumerate(grads):
        specs += [resident(part) for part in grad]
        flat += grad
        if weights:
            weight, start = weights[index]
            block = (grad[0].shape[1], tile)
            specs.append(pl.BlockSpec(block, lambda i, start=start: (start, i)))
            flat.append(weight)
    return call(
        functools.partial(
            weight_grad_kernel, groups=len(rows), parts=len(grads[0]), summed=bool(weights)
        ),
        "weight_grad",
        4,
        specs,
        [pl.BlockSpec((columns, tile), lambda i: (0, i))]
        + ([pl.BlockSpec((8, tile), lambda i: (0, i))] if weights else []),
        [jax.ShapeDtypeStruct((columns, width), BF)]
        + ([jax.ShapeDtypeStruct((8, width), F32)] if weights else []),
        2 * count * width * columns,
    )(*flat)


def norm_back_kernel(sum_ref, x_ref, y_ref, values_ref, base_ref, gain_ref, out_ref, low_ref):
    values = values_ref[...].astype(F32)
    width = values.shape[1]
    grad = sum_ref[...] + x_ref[...].astype(F32) + y_ref[...].astype(F32)
    inverse = lax.rsqrt(jnp.sum(values * values, axis=-1, keepdims=True) / width + EPS)
    gained = grad * gain_ref[...]
    inner = jnp.sum(gained * values, axis=-1, keepdims=True)
    scale = inverse * inverse * inverse * inner / width
    total = base_ref[...].astype(F32) + inverse * gained - values * scale
    out_ref[...] = total
    low_ref[...] = total.astype(BF)


def norm_back(own, received, values, base, gain):
    rows, width = values.shape
    tile = row_tile(rows // 4, width)
    return call(
        norm_back_kernel,
        "norm_back",
        4,
        [tile] * 5 + [resident(gain)],
        [tile, tile],
        [jax.ShapeDtypeStruct((rows, width), F32), jax.ShapeDtypeStruct((rows, width), BF)],
        1000 * rows * width,
    )(own, *received, values, base, gain)


def out_grad_kernel(*refs, small):
    rows_ref, grads, out_ref = refs[0], refs[1:-1], refs[-1]
    product, place = 0.0, 0
    for grad_ref in grads:
        count = grad_ref.shape[0]
        product = product + tn(rows_ref[place : place + count, :], grad_ref[...])
        place += count
    product = product.astype(BF)
    tile = product.shape[1]
    for group in range(product.shape[0] // small):
        out_ref[:, group * tile : (group + 1) * tile] = product[group * small : (group + 1) * small]


def out_grad(rows, grads, small, pieces):
    count, columns = rows.shape
    width = grads[0].shape[1]
    tile = width // pieces
    return call(
        functools.partial(out_grad_kernel, small=small),
        "out_grad",
        pieces,
        [resident(rows)] + [pl.BlockSpec((grad.shape[0], tile), lambda i: (0, i)) for grad in grads],
        row_tile(small, columns // small * tile),
        jax.ShapeDtypeStruct((pieces * small, columns // small * tile), BF),
        2 * count * width * columns,
    )(rows, *grads)


def per_device(
    residual,
    cotangent,
    attn_gain,
    query_weight,
    key_weight,
    value_weight,
    out_weight,
    ffn_gain,
    gate_weight,
    up_weight,
    down_weight,
):
    dp_size = lax.axis_size("dp")
    seq_size = lax.axis_size("seq")
    count = dp_size * seq_size
    planes = dp_size // 2
    rank = lax.axis_index("seq")
    is_first = lax.axis_index("dp") % 2 == 0
    first_core = rank % 2 == 0
    place = jnp.full((1,), rank, jnp.int32)
    tokens = residual.shape[1]
    width = residual.shape[2]
    small = query_weight.shape[0]
    rows_ffn = gate_weight.shape[0]
    head_cols = query_weight.shape[1] // 8
    hidden_half = gate_weight.shape[1] // 2

    out_moves = [(k, (k % planes) * 8 + k // planes) for k in range(count)]
    plane_out = lax.ppermute(out_weight, AXES, out_moves)

    own_kv = jnp.stack(
        [key_weight.reshape(small, 4, HD), value_weight.reshape(small, 4, HD)], axis=2
    ).reshape(small, 8, HD)
    gains = jnp.pad(jnp.stack([attn_gain, ffn_gain], axis=1), ((0, 0), (0, EXTRA - 2)))
    gains = jnp.broadcast_to(gains[:, None], (small, 8, EXTRA))
    send = jnp.concatenate([query_weight.reshape(small, 8, head_cols), own_kv, gains], axis=2)
    plane_qkv = exchange_plane(send.swapaxes(0, 1)).reshape(8 * small, -1).T
    pieces = width // (8 * small)

    def pack_out(rows):
        return rows.reshape(small, pieces, 8 * small).swapaxes(0, 1).reshape(pieces * small, -1)

    def unpack_out(rows, groups):
        blocks = rows.reshape(pieces, small, groups, 8 * small)
        return blocks.transpose(2, 1, 0, 3).reshape(groups * small, -1)

    own_packed = jnp.concatenate(
        [plane_qkv[:head_cols], pack_out(plane_out), plane_qkv[head_cols:]], axis=0
    )
    packed = gather_z(own_packed)

    def halves(weights):
        parts = [(w[:hidden_half], w[hidden_half:]) for w in weights]
        mine = jnp.concatenate([jnp.where(is_first, left, right) for left, right in parts], axis=0)
        theirs = jnp.concatenate([jnp.where(is_first, right, left) for left, right in parts], axis=0)
        return jnp.concatenate(pick(is_first, mine, flip(theirs, 4)), axis=1)

    half_two = halves([gate_weight.T, up_weight.T])
    tables = rotary_tables(tokens * seq_size)
    row_groups = gather_plane(after(residual[0], own_packed), before=(half_two, tables))[0]
    w_two = gather_z(after(half_two, packed))
    cot_rows = cotangent[0]
    half = tokens // 2
    cot_early = after(cot_rows, *row_groups[2][:2])
    cot_y = flip(cot_early, 2)
    cot_x = flip(cot_early, 4)
    packed, row_groups = lax.optimization_barrier((packed, row_groups))

    w_out = unpack_out(packed[head_cols : 2 * head_cols], planes)
    own_half = packed[2 * head_cols : 2 * head_cols + HD]
    gain_row = 2 * head_cols + HD
    gain_one = packed[gain_row : gain_row + 1].astype(F32)
    gain_two = packed[gain_row + 1 : gain_row + 2].astype(F32)
    nothing = jnp.zeros_like(own_half)
    w_kv = jnp.concatenate(
        [jnp.where(first_core, own_half, nothing), jnp.where(first_core, nothing, own_half)], axis=0
    )
    row_pieces = row_groups[0] + row_groups[1] + row_groups[2]
    normed_one, queries, kv = project(row_pieces, gain_one, packed, w_kv)
    kv_other = flip(kv, 1)
    attended, lse = attend(queries, kv, kv_other, tables, place)
    half_down = halves([after(down_weight, queries).T])
    w_down = gather_z(half_down)
    attended, cot_y, cot_x = lax.optimization_barrier((attended, cot_y, cot_x, half_down))[:3]

    def scatter_rows(rows, weight):
        block = lambda i: nn(rows[i * tokens : (i + 1) * tokens], weight).astype(BF)
        theirs = block(7)
        relayed = scatter_relay((block(6), theirs))
        rows = after(rows, relayed[2])
        theirs = (block(3), block(5))
        chip_y, chip_x = chip_sum((block(2), theirs[0])), chip_sum((block(4), theirs[1]))
        sent = scatter_middle(chip_y, chip_x, relayed)
        rows = after(rows, *sent)
        theirs = block(1)
        return (sent, chip_sum((block(0), theirs)))

    sent, own = scatter_rows(attended, w_out)
    cot_own = [after(cot_rows, *sent), flip(after(cot_rows, *sent), 1)]
    cot_near = [cot_y, flip(cot_y, 1), cot_x, flip(cot_x, 1)]
    cots = [jnp.concatenate(cot_own, axis=0), jnp.concatenate(cot_near, axis=0)]
    received = scatter_end(sent)
    branch = own + received[0].astype(F32) + received[1].astype(F32)
    branch, cots = lax.optimization_barrier((branch, cots))
    stream = residual[0].astype(F32)
    middle = stream + branch
    inverse_two = lax.rsqrt(jnp.mean(middle * middle, axis=-1, keepdims=True) + EPS)

    squares = [jnp.sum(rows * rows) for rows in (stream, branch)]
    groups, results = gather_plane(
        (middle * inverse_two * gain_two).astype(BF),
        lambda group, _: ffn_hidden(group, w_two, tokens),
        tuple(squares),
    )
    normed_two, hidden, by_gate, by_up = zip(*results)
    cot_top, cot_low = lax.optimization_barrier((cot_x[:half], cot_y[half:], groups[2][:2]))[:2]
    cot_far = lax.optimization_barrier(((flip(cot_top, 2), flip(cot_low, 4)), hidden[2]))[0]
    cot_far = list(cot_far)
    cots.append(jnp.concatenate(cot_far + [flip(piece, 1) for piece in cot_far], axis=0))
    term_down = weight_grad(cots, hidden)[0]
    sum_down = scatter_z(term_down)

    def back(which, *others):
        groups = [(cots[i], by_gate[i], by_up[i]) for i in which]
        groups = lax.optimization_barrier((groups, term_down, others))[0]
        return ffn_back(groups, w_down, w_two, tokens)

    gate_outer, up_outer, *parts = back((1, 2))
    relayed = scatter_relay(parts[2:])
    gate_own, up_own, *own = back((0,), relayed[2])
    chip = chip_sum(parts[:2])
    sent = scatter_middle(chip[:tokens], chip[tokens:], relayed)
    kept = lax.optimization_barrier((normed_two, sent))[0]
    kept = list(kept)
    term_two, gain_sum_two = weight_grad(
        kept, [gate_own, gate_outer], [up_own, up_outer], weights=[(w_two, 0), (w_two, 1)]
    )
    sum_two = scatter_z(term_two)
    received = lax.optimization_barrier((scatter_end(sent), term_two))[0]
    own = chip_sum(own, *received)

    def own_rows(term):
        first, second = term[:, :rows_ffn], term[:, rows_ffn:]
        other = flip(jnp.where(is_first, second, first), 4)
        return pick(is_first, jnp.where(is_first, first, second), other)

    grad_middle, grad_branch = norm_back(own, received, middle, cot_rows, gain_two)
    whole = jnp.zeros(attended.shape, BF)
    feed_near = split_product(after(hidden[1], grad_middle), w_down, tokens, 0, 4)
    feed_far = split_product(after(hidden[2], grad_middle), w_down, tokens, 0, 2)
    groups = gather_plane(grad_branch, before=(feed_near, feed_far))[0]
    feed_own = split_product(after(hidden[0], feed_near, feed_far, sum_down), w_down, tokens, 0, 2)

    w_out = lax.optimization_barrier((w_out, feed_own))[0]
    near, whole = gathered_dot(groups[0] + groups[1], w_out, 0, whole)
    far, whole = gathered_dot(groups[2], w_out, 6, whole)
    grad_branch = [near, far]
    relayed = scatter_relay(feed_far)
    term_out = out_grad(attended, grad_branch, small, pieces)
    relayed = lax.optimization_barrier((relayed, term_out))[0]
    chip = chip_sum(feed_near)
    feed_sent = scatter_middle(chip[:tokens], chip[tokens:], relayed)
    down_first, down_second = own_rows(sum_down)
    grad_down_w = jnp.concatenate([down_first, down_second], axis=0).T.astype(F32)
    whole, feed_sent = lax.optimization_barrier((whole, feed_sent, term_out, down_second))[:2]
    feed_received = scatter_end(feed_sent)
    grad_q, grad_kv = attend_back(queries, kv, kv_other, whole, lse, tables, place)
    grad_q, grad_kv, feed_received = lax.optimization_barrier((grad_q, grad_kv, feed_received))
    kv_back = flip(grad_kv, 1)
    kv_back = kv_back.reshape(4, 2, tokens, -1)[:, ::-1].reshape(kv_back.shape)
    grad_kv = (grad_kv + kv_back).astype(BF)
    term_qkv, gain_sum_one = weight_grad([normed_one], [grad_q], [grad_kv], weights=[(packed, 0), (w_kv, 0)])
    key_row = head_cols + HD
    value_row = key_row + HD
    term_kv = jnp.where(first_core, term_qkv[head_cols:key_row], term_qkv[key_row:value_row])
    feed = chip_sum(feed_own) + feed_received[0].astype(F32) + feed_received[1].astype(F32)
    total_out = middle + feed
    squares = squares + [jnp.sum(rows * rows) for rows in (feed, total_out)]
    extra = -(-(4 * planes + 2) // EXTRA) * EXTRA
    column = lax.broadcasted_iota(jnp.int32, (extra, width), 1) % small
    row = lax.broadcasted_iota(jnp.int32, (extra, width), 0)
    spread = sum(jnp.where(column == k, squares[k], 0.0) for k in range(4))
    riders = jnp.zeros((extra, width), F32)
    first = lax.axis_index("dp") // 2 * 4
    for start, value in (
        (first, gain_sum_one[:1]),
        (first + 2, gain_sum_two[:1]),
        (4 * planes, spread),
    ):
        high = lax.reduce_precision(value, 8, 7)
        riders = jnp.where(row == start, high, jnp.where(row == start + 1, value - high, riders))
    term_qkv = jnp.concatenate(
        [term_qkv[:head_cols], term_out, term_kv, riders.astype(BF)], axis=0
    )
    sums = scatter_z(after(term_qkv, sum_two))
    late_q, late_kv = lax.optimization_barrier((grad_q, grad_kv, term_qkv))[:2]
    late = jnp.concatenate([late_q, late_kv], axis=1)
    w_qkv = jnp.concatenate([packed[:head_cols], w_kv], axis=0)
    sent, own = scatter_rows(late, w_qkv)
    received = scatter_end(sent)
    two_first, two_second = own_rows(after(sum_two, *received))
    grad_stream = norm_back(own, received, residual[0], grad_middle, gain_one)[0]

    grad_gate_w = jnp.concatenate([two_first[:hidden_half], two_second[:hidden_half]], axis=0).T
    grad_up_w = jnp.concatenate([two_first[hidden_half:], two_second[hidden_half:]], axis=0).T
    grad_gate_w, grad_up_w = grad_gate_w.astype(F32), grad_up_w.astype(F32)
    sums, total_out, grad_down_w = lax.optimization_barrier((sums, total_out, grad_down_w))

    plane_grad = jnp.concatenate(
        [sums[:head_cols], sums[2 * head_cols :]], axis=0
    ).T
    back = exchange_plane(plane_grad.reshape(8, small, -1))
    grad_out_rows = unpack_out(sums[head_cols : 2 * head_cols], 1)
    grad_out_w = lax.ppermute(grad_out_rows, AXES, [(b, a) for a, b in out_moves]).astype(F32)
    back = back.swapaxes(0, 1).astype(F32)
    row_sums = jnp.sum(back[:, :, head_cols + HD :], axis=1)
    rms_stats = jnp.sqrt(
        jnp.sum(row_sums[:4, 4 * planes : 4 * planes + 2], axis=1) / (tokens * count * width)
    )
    gain_sums = jnp.sum(row_sums[:, : 4 * planes].reshape(small, planes, 2, 2), axis=(1, 3))
    grad_attn_gain = gain_sums[:, 0] / attn_gain.astype(F32)
    grad_ffn_gain = gain_sums[:, 1] / ffn_gain.astype(F32)
    back_kv = back[:, :, head_cols : head_cols + HD].reshape(small, 4, 2, HD)
    return (
        total_out.astype(BF)[None],
        grad_stream[None],
        grad_attn_gain,
        back[:, :, :head_cols].reshape(small, -1),
        back_kv[:, :, 0].reshape(small, -1),
        back_kv[:, :, 1].reshape(small, -1),
        grad_out_w,
        grad_ffn_gain,
        grad_gate_w,
        grad_up_w,
        grad_down_w,
        rms_stats,
    )


def solution(mesh):
    token_spec = P("dp", "seq", None)
    gain_spec = P(("dp", "seq"))
    row_spec = P(("dp", "seq"), None)
    ffn_spec = P("dp", "seq")
    weight_specs = (gain_spec, row_spec, row_spec, row_spec, row_spec, gain_spec) + (ffn_spec,) * 3
    return jax.shard_map(
        per_device,
        mesh=mesh,
        in_specs=(token_spec, token_spec) + weight_specs,
        out_specs=(token_spec, token_spec) + weight_specs + (P(),),
        check_vma=False,
    )
```
